128 devices in a mesh: ctx: 32 (over y, z, core), fsdp: 4 (over x).
Axes of the slice: x: 4, y: 4, z: 4, core: 2. Of those that a mesh axis runs over, the one named last changes fastest.
Arguments:
- gate_in: bfloat16 [16384, 4096], P('ctx', 'fsdp'), may hold values from -6 to 6
- values: bfloat16 [16384, 4096], P('ctx', 'fsdp'), may hold values from -6 to 6
- gate_out: bfloat16 [16384, 4096], P('ctx', 'fsdp'), may hold values from -6 to 6
- bias: float32 [4096], P('fsdp'), may hold values from -4 to 4
- spectrum: bfloat16 [2, 32768, 4096], P(None, ('ctx', 'fsdp')), may hold values from -6 to 6
Outputs:
- gated: bfloat16 [16384, 4096], P('ctx', 'fsdp')
The draws below stay inside these ranges and needn't reach their ends.
All inputs are finite; a program needn't handle non-finite values.
Results may differ from the reference program's by a relative error of at most 0.0049.
Values may be sent and summed in bfloat16 or wider, within the bound.
No kernel may reach another device: no remote copies, remote signals or barrier semaphores. Data moves between devices by JAX's collectives and lax.ppermute only.
A program may use at most 128 MiB of HBM per device.

```python
import jax
import jax.numpy as jnp
from jax import lax

D = 4096
TOK_DEV = 512
SEQ = 16384
FREQ = 32768
RADIX = 64
N_CTX = 32
N_FSDP = 4


def block_levels(stream_key, dims, cuts, least, largest):
    loudness = 1.0
    for dim, blocks in cuts:
        steps = jax.random.uniform(jax.random.fold_in(jax.random.fold_in(stream_key, 6), dim), (blocks,), jnp.float32, least / len(cuts), largest / len(cuts))
        loudness = loudness * jnp.repeat(jnp.exp(steps), dims[dim] // blocks).reshape((-1,) + (1,) * (len(dims) - 1 - dim))
    return loudness


def noise(key, shape, spread, reach, cuts=(), held_as=jnp.bfloat16):
    result = jax.random.normal(key, shape, jnp.float32) * spread
    if len(cuts) > 0:
        result = block_levels(key, shape, cuts, -0.22, 0.18) * result
    return jnp.clip(result, min=-reach, max=reach).astype(held_as)


def setup_inputs(seed: int = 0) -> dict:
    seeds = jax.random.split(jax.random.key(seed), 6)
    gate_in = noise(seeds[0], (SEQ, D), 1.0, 6.0, ((0, 32), (1, 4)))
    values = noise(seeds[1], (SEQ, D), 1.0, 6.0, ((0, 32), (1, 4)))
    gate_out = noise(seeds[2], (SEQ, D), 1.0, 6.0, ((0, 32), (1, 4)))
    bias = noise(seeds[3], (D,), 1.0, 4.0, ((0, 4),), jnp.float32)
    spectrum = noise(seeds[4], (2, FREQ, D), 1.0, 6.0, ((1, 128),))
    return {"gate_in": gate_in, "values": values, "gate_out": gate_out, "bias": bias, "spectrum": spectrum}


def reference(gate_in, values, gate_out, bias, spectrum):
    length = TOK_DEV * N_CTX
    frequency = jnp.arange(FREQ, dtype=jnp.int32)
    residue = (frequency % RADIX).astype(jnp.int32)
    half_radix = RADIX // 2
    slot_number = (residue >= half_radix).astype(jnp.int32)
    owner = jnp.where(residue < half_radix, residue, jnp.where(residue == half_radix, 0, RADIX - residue)).astype(jnp.int32)
    storage_row = (owner * (2 * TOK_DEV) + slot_number * TOK_DEV + frequency // RADIX).astype(jnp.int32)
    width_block = D // N_FSDP
    outputs = []
    for block_number in range(N_FSDP):
        low_col = block_number * width_block
        high_col = low_col + width_block
        product_in = (gate_in[:, low_col:high_col].astype(jnp.float32) * values[:, low_col:high_col].astype(jnp.float32)).astype(jnp.bfloat16)
        product_in = lax.optimization_barrier(product_in)
        signal = product_in.astype(jnp.float32)
        padded = jnp.concatenate([signal, jnp.zeros_like(signal)], axis=0)
        transformed = jnp.fft.fft(padded, axis=0)
        filter_real = jnp.take(spectrum[0, :, low_col:high_col], storage_row, axis=0).astype(jnp.float32)
        filter_imag = jnp.take(spectrum[1, :, low_col:high_col], storage_row, axis=0).astype(jnp.float32)
        response = lax.complex(filter_real, filter_imag)
        convolved = jnp.real(jnp.fft.ifft(transformed * response, axis=0))[:length]
        convolved = convolved + bias[low_col:high_col][None, :] * signal
        outputs.append((gate_out[:, low_col:high_col].astype(jnp.float32) * convolved).astype(jnp.bfloat16))
    return jnp.concatenate(outputs, axis=1)
```

```python
import functools
import math

import jax
import jax.numpy as jnp
from jax import lax
from jax.experimental import pallas as pl
from jax.experimental.pallas import tpu as pltpu
from jax.sharding import PartitionSpec as P

CHUNKS = 1
LANES = 256


def cosine(step, modulus):
    half = modulus // 2
    centred = jnp.bitwise_and(step + half, modulus - 1) - half
    y = (modulus // 4 - jnp.abs(centred)).astype(jnp.float32) * (2.0 * math.pi / modulus)
    z = y * y
    series = 1.0 / 6227020800.0
    for term in (-1.0 / 39916800.0, 1.0 / 362880.0, -1.0 / 5040.0, 1.0 / 120.0, -1.0 / 6.0, 1.0):
        series = series * z + term
    return series * y


def split(table):
    high = lax.reduce_precision(table, 8, 7)
    return high.astype(jnp.bfloat16), (table - high).astype(jnp.bfloat16)


def cross_table(devices, block, transpose, scale):
    wide = jnp.arange(2 * devices * block, dtype=jnp.int32)
    residue, part, wide_row = wide // (2 * block), (wide // block) % 2, wide % block
    narrow = jnp.arange(devices * block, dtype=jnp.int32)
    place, narrow_row = narrow // block, narrow % block
    first = residue == 0
    rate = jnp.where(first, part * devices, residue)
    phase = jnp.where(first, 0, part * (devices // 2))
    if transpose:
        step = place[:, None] * rate[None, :] + phase[None, :]
        same = narrow_row[:, None] == wide_row[None, :]
    else:
        step = rate[:, None] * place[None, :] + phase[:, None]
        same = wide_row[:, None] == narrow_row[None, :]
    return split(jnp.where(same, cosine(step, 2 * devices) * scale, 0.0))


def local_table(position, devices, rows, block, transpose):
    length = 2 * devices * rows
    stride = 2 * devices
    half = rows // 2
    first = position == 0
    out = jnp.arange(2 * rows, dtype=jnp.int32)
    out_part, order = out // rows, out % rows
    upper = (order >= half).astype(jnp.int32)
    packed_rate = jnp.where(
        order == 0, out_part * half * stride, stride * (order - upper * half) + upper * devices
    )
    rate = jnp.where(first, packed_rate, stride * order + position)
    out_phase = jnp.where(first & (order == 0), 0, out_part)
    inp = jnp.arange(2 * rows, dtype=jnp.int32)
    in_part = (inp // block) % 2
    row = (inp // (2 * block)) * block + inp % block
    in_phase = jnp.where(first, 0, in_part)
    out_side = jnp.where(first, upper, 2)
    quarter = length // 4
    if transpose:
        step = row[:, None] * rate[None, :] + quarter * (out_phase[None, :] - in_phase[:, None])
        keep = (out_side[None, :] == 2) | (out_side[None, :] == in_part[:, None])
    else:
        step = rate[:, None] * row[None, :] + quarter * (out_phase[:, None] - in_phase[None, :])
        keep = (out_side[:, None] == 2) | (out_side[:, None] == in_part[None, :])
    return split(jnp.where(keep, cosine(step, length), 0.0))


def filter_tables(position, member, members, rows):
    first = position == 0
    half = rows // 2
    out = jnp.arange(rows + 8, dtype=jnp.int32)
    order = jnp.minimum(out, rows - 1)
    body = out < rows
    upper = order >= half
    here = jnp.where(first, jnp.where(upper, rows + order - half, order), order)
    there = jnp.where(
        first,
        jnp.where(upper, 2 * rows - 1 - (order - half), (rows - order) % rows),
        2 * rows - 1 - order,
    )
    edge = first & (order == 0)
    stored = jnp.arange(2 * rows, dtype=jnp.int32)
    part = 2 * rows // members
    stored = (member + members - stored // part) % members * part + stored % part
    hit_here = (stored[None, :] == here[:, None]).astype(jnp.float32)
    hit_there = (stored[None, :] == there[:, None]).astype(jnp.float32)
    weight = jnp.where(edge, 0.25, 0.5)[:, None]
    even = weight * (hit_here + hit_there)
    odd = weight * (hit_here - hit_there)
    fix = 0.5 * ((stored[None, :] == half).astype(jnp.float32) - (stored[None, :] == 0).astype(jnp.float32))
    fix = jnp.where(first & (out[:, None] == rows), fix, 0.0)
    even = jnp.where(body[:, None], even, fix)
    return even.astype(jnp.bfloat16), odd[:rows].astype(jnp.bfloat16)


def dot(a, b):
    return jnp.dot(a, b, preferred_element_type=jnp.float32)


def cross_kernel(high_ref, low_ref, x_ref, o_ref):
    x = x_ref[...]
    o_ref[...] = (dot(high_ref[...], x) + dot(low_ref[...], x)).astype(o_ref.dtype)


def filter_kernel(even_ref, odd_ref, *refs):
    *pieces, even_out, odd_out = refs
    rows = pieces[0].shape[1]
    even = odd = 0.0
    for shift, piece in enumerate(pieces):
        cols = slice(shift * rows, (shift + 1) * rows)
        even += dot(even_ref[:, cols], piece[0])
        odd += dot(odd_ref[:, cols], piece[1])
    even_out[...] = even
    odd_out[...] = odd


def local_kernel(fh_ref, fl_ref, gh_ref, gl_ref, even_ref, odd_ref, x_ref, o_ref):
    rows = odd_ref.shape[0]
    x = x_ref[...]
    freq = dot(fh_ref[...], x) + dot(fl_ref[...], x)
    real, imag = freq[:rows], freq[rows:]
    even, odd = even_ref[:rows], odd_ref[...]
    prod_real = real * even - imag * odd
    prod_imag = real * odd + imag * even
    edge = prod_imag[:8] + imag[:8] * even_ref[rows:]
    prod = jnp.concatenate([prod_real, edge, prod_imag[8:]], axis=0).astype(jnp.bfloat16)
    o_ref[...] = (dot(gh_ref[...], prod) + dot(gl_ref[...], prod)).astype(o_ref.dtype)


def whole(array):
    return pl.BlockSpec(array.shape, lambda i: (0,) * array.ndim)


def columns(shape):
    return pl.BlockSpec(shape[:-1] + (LANES,), lambda i: (0,) * (len(shape) - 1) + (i,))


def call(kernel, tables, streams, outs, name):
    many = isinstance(outs, tuple)
    width = streams[0].shape[-1]
    return pl.pallas_call(
        kernel,
        grid=(width // LANES,),
        in_specs=[whole(t) for t in tables] + [columns(s.shape) for s in streams],
        out_specs=tuple(columns(o.shape) for o in outs) if many else columns(outs.shape),
        out_shape=outs,
        name=name,
    )(*tables, *streams)


def exchange(array):
    return lax.all_to_all(array, "ctx", split_axis=0, concat_axis=0, tiled=True)


def body(gate_in, values, gate_out, bias, spectrum):
    devices = lax.axis_size("ctx")
    members = lax.axis_size("fsdp")
    rows, channels = gate_in.shape
    block = rows // devices
    length = 2 * rows * devices
    width = channels // CHUNKS
    position = lax.axis_index("ctx")
    shape = jax.ShapeDtypeStruct

    def cols(array, c):
        return array[..., c * width : (c + 1) * width]

    mixed = [
        (cols(gate_in, c).astype(jnp.float32) * cols(values, c).astype(jnp.float32)).astype(jnp.bfloat16)
        for c in range(CHUNKS)
    ]
    mixed = lax.optimization_barrier(mixed)
    stage1 = [exchange(m.reshape(devices, block, width)).reshape(rows, width) for m in mixed]

    member = lax.axis_index("fsdp")
    held = []
    for shift in range(members):
        target = lax.rem(member + shift, members)
        piece = lax.dynamic_slice_in_dim(spectrum, target * channels, channels, 2)
        if shift > 0:
            ring = [(m, (m + shift) % members) for m in range(members)]
            piece = lax.ppermute(piece, "fsdp", ring)
        held.append(piece)

    cross = cross_table(devices, block, False, 1.0)
    cross_back = cross_table(devices, block, True, 2.0 / length)
    local = local_table(position, devices, rows, block, False)
    local_back = local_table(position, devices, rows, block, True)
    even_table, odd_table = filter_tables(position, member, members, rows)
    even, odd = call(
        filter_kernel,
        (even_table, odd_table),
        held,
        (shape((rows + 8, channels), jnp.float32), shape((rows, channels), jnp.float32)),
        "filters",
    )

    stage2 = []
    for c in range(CHUNKS):
        spread = call(cross_kernel, cross, (stage1[c],), shape((2 * rows, width), jnp.bfloat16), "cross")
        stage2.append(exchange(spread.reshape(devices, 2 * block, width)).reshape(2 * rows, width))
    stage3 = []
    for c in range(CHUNKS):
        turned = call(
            local_kernel,
            local + local_back,
            (cols(even, c), cols(odd, c), stage2[c]),
            shape((2 * rows, width), jnp.bfloat16),
            "local",
        )
        stage3.append(exchange(turned.reshape(devices, 2 * block, width)).reshape(2 * rows, width))
    outs = []
    for c in range(CHUNKS):
        folded = call(cross_kernel, cross_back, (stage3[c],), shape((rows, width), jnp.bfloat16), "fold")
        restored = exchange(folded.reshape(devices, block, width)).reshape(rows, width)
        convolved = restored.astype(jnp.float32) + cols(bias, c)[None, :] * mixed[c].astype(jnp.float32)
        outs.append((cols(gate_out, c).astype(jnp.float32) * convolved).astype(jnp.bfloat16))
    return jnp.concatenate(outs, axis=1)


def solution(mesh):
    return jax.shard_map(
        body,
        mesh=mesh,
        in_specs=(
            P("ctx", "fsdp"),
            P("ctx", "fsdp"),
            P("ctx", "fsdp"),
            P("fsdp"),
            P(None, ("ctx", "fsdp"), None),
        ),
        out_specs=P("ctx", "fsdp"),
        check_vma=False,
    )
```

```python
import math

import jax
import jax.numpy as jnp
from jax import lax
from jax.experimental import pallas as pl
from jax.experimental.pallas import tpu as pltpu
from jax.sharding import PartitionSpec as P


LANES = 256
RADIX = 4


def cosine(step, modulus):
    half = modulus // 2
    centred = jnp.bitwise_and(step + half, modulus - 1) - half
    y = (modulus // 4 - jnp.abs(centred)).astype(jnp.float32) * (2.0 * math.pi / modulus)
    z = y * y
    series = 1.0 / 6227020800.0
    for term in (-1.0 / 39916800.0, 1.0 / 362880.0, -1.0 / 5040.0, 1.0 / 120.0, -1.0 / 6.0, 1.0):
        series = series * z + term
    return series * y


def split(table):
    high = lax.reduce_precision(table, 8, 7)
    return high.astype(jnp.bfloat16), (table - high).astype(jnp.bfloat16)


def message(index, block):
    fine = block // RADIX
    return index % fine * RADIX + index // (2 * fine) % RADIX, index // fine % 2


def cross_table(devices, block, transpose, scale):
    wide = jnp.arange(2 * devices * block, dtype=jnp.int32)
    residue = wide // (2 * block)
    wide_row, part = message(wide, block)
    narrow = jnp.arange(devices * block, dtype=jnp.int32)
    place, narrow_row = narrow // block, narrow % block
    first = residue == 0
    rate = jnp.where(first, part * devices, residue)
    phase = jnp.where(first, 0, part * (devices // 2))
    if transpose:
        step = place[:, None] * rate[None, :] + phase[None, :]
        same = narrow_row[:, None] == wide_row[None, :]
    else:
        step = rate[:, None] * place[None, :] + phase[:, None]
        same = wide_row[:, None] == narrow_row[None, :]
    return split(jnp.where(same, cosine(step, 2 * devices) * scale, 0.0))


def local_table(position, devices, rows, block, transpose):
    length = 2 * devices * rows
    stride = 2 * devices
    fine = block // RADIX
    quart = rows // RADIX
    first = position == 0
    out = jnp.arange(4 * quart, dtype=jnp.int32)
    group, out_part, order = out // (2 * quart), out // quart % 2, out % quart
    rate = jnp.where(first, stride * order + group * devices, stride * (order + 2 * quart * group) + position)
    inp = jnp.arange(2 * devices * fine, dtype=jnp.int32)
    in_part = inp // fine % 2
    base = inp // (2 * fine) * block + inp % fine * RADIX
    in_phase = jnp.where(first, 0, in_part)
    side = jnp.where(first, group, 2)
    digit = jnp.arange(RADIX, dtype=jnp.int32)[:, None, None]
    quarter = length // 4
    if transpose:
        row = digit + base[None, :, None]
        step = row * rate[None, None, :] + quarter * (out_part[None, None, :] - in_phase[None, :, None])
        keep = (side[None, :] == 2) | (side[None, :] == in_part[:, None])
    else:
        row = digit + base[None, None, :]
        step = row * rate[None, :, None] + quarter * (out_part[None, :, None] - in_phase[None, None, :])
        keep = (side[:, None] == 2) | (side[:, None] == in_part[None, :])
    return split(jnp.where(keep[None], cosine(step, length), 0.0))


def filter_tables(position, member, members, rows):
    first = position == 0
    half = rows // 2
    out = jnp.arange(rows + 8, dtype=jnp.int32)
    order = jnp.minimum(out, rows - 1)
    upper = order >= half
    here = jnp.where(first, jnp.where(upper, rows + order - half, order), order)
    there = jnp.where(
        first,
        jnp.where(upper, 2 * rows - 1 - (order - half), (rows - order) % rows),
        2 * rows - 1 - order,
    )
    stored = jnp.arange(2 * rows, dtype=jnp.int32)
    part = 2 * rows // members
    stored = (member + members - stored // part) % members * part + stored % part
    hit_here = (stored[None, :] == here[:, None]).astype(jnp.float32)
    hit_there = (stored[None, :] == there[:, None]).astype(jnp.float32)
    weight = jnp.where(first & (order == 0), 0.25, 0.5)[:, None]
    even = weight * (hit_here + hit_there)
    odd = weight * (hit_here - hit_there)
    edge = jnp.where(first & (out[:, None] == rows) & (stored[None, :] == half), 0.5, 0.0)
    even = jnp.where((out < rows)[:, None], even, edge)
    return even.astype(jnp.bfloat16), odd[:rows].astype(jnp.bfloat16)


def dot(high, low, x):
    return jnp.dot(
        jnp.concatenate([high, low], axis=1),
        jnp.concatenate([x, x], axis=0),
        preferred_element_type=jnp.float32,
    )


def each_block(width, step):
    def go(i, carry):
        step(pl.ds(pl.multiple_of(i * LANES, LANES), LANES))
        return carry

    lax.fori_loop(0, width // LANES, go, 0)


def cross_kernel(high_ref, low_ref, x_ref, o_ref):
    def step(cols):
        o_ref[:, cols] = dot(high_ref[...], low_ref[...], x_ref[:, cols]).astype(o_ref.dtype)

    each_block(x_ref.shape[1], step)


def filter_kernel(even_ref, odd_ref, *refs):
    *pieces, even_out, odd_out = refs
    rows = pieces[0].shape[1]
    even = odd = 0.0
    for shift, piece in enumerate(pieces):
        cols = slice(shift * rows, (shift + 1) * rows)
        even += jnp.dot(even_ref[:, cols], piece[0], preferred_element_type=jnp.float32)
        odd += jnp.dot(odd_ref[:, cols], piece[1], preferred_element_type=jnp.float32)
    even_out[...] = even
    odd_out[...] = odd


def local_kernel(mh_ref, ml_ref, gh_ref, gl_ref, even_ref, odd_ref, x_ref, o_ref):
    rows = odd_ref.shape[0]
    quart = rows // RADIX

    def step(cols):
        v = []
        for digit in range(RADIX):
            x = x_ref[:, digit, :, cols]
            v.append(dot(mh_ref[digit], ml_ref[digit], x.reshape(-1, x.shape[-1])))
        sum02, sum13, gap02, gap13 = v[0] + v[2], v[1] + v[3], v[0] - v[2], v[1] - v[3]
        edge = (sum02[:8] - sum13[:8]) * even_ref[rows:, cols]
        total = sum02 + sum13
        packed = [[] for _ in range(RADIX)]
        for group in range(2):
            at = 2 * group * quart
            re, im = slice(at, at + quart), slice(at + quart, at + 2 * quart)
            parts = []
            for turn, (real, imag) in enumerate(
                ((total[re], total[im]), (gap02[re] + gap13[im], gap02[im] - gap13[re]))
            ):
                here = pl.ds(at + turn * quart, quart)
                even, odd = even_ref[here, cols], odd_ref[here, cols]
                parts.append((real * even - imag * odd, real * odd + imag * even))
            (r0, i0), (r1, i1) = parts
            for digit, (real, imag) in enumerate(
                ((r0 + r1, i0 + i1), (r0 - i1, i0 + r1), (r0 - r1, i0 - i1), (r0 + i1, i0 - r1))
            ):
                if group == 0:
                    top = real[:8] + edge if digit % 2 == 0 else real[:8] - edge
                    packed[digit].append(jnp.concatenate([top, real[8:]], axis=0))
                else:
                    packed[digit].append(real)
                packed[digit].append(imag)
        for digit in range(RADIX):
            b = jnp.concatenate(packed[digit], axis=0).astype(jnp.bfloat16)
            y = dot(gh_ref[digit], gl_ref[digit], b)
            o_ref[:, digit, :, cols] = y.reshape(o_ref.shape[0], o_ref.shape[2], -1).astype(o_ref.dtype)

    each_block(odd_ref.shape[1], step)


def call(kernel, operands, outs, grant):
    vmem = pl.BlockSpec(memory_space=pltpu.VMEM)
    return pl.pallas_call(
        kernel,
        in_specs=[vmem] * len(operands),
        out_specs=vmem,
        out_shape=outs,
        compiler_params=pltpu.CompilerParams(vmem_limit_bytes=grant << 20),
    )(*operands)


def exchange(array):
    return lax.all_to_all(array, "ctx", split_axis=0, concat_axis=0, tiled=True)


def body(gate_in, values, gate_out, bias, spectrum):
    devices = lax.axis_size("ctx")
    members = lax.axis_size("fsdp")
    rows, channels = gate_in.shape
    block = rows // devices
    length = 2 * rows * devices
    position = lax.axis_index("ctx")
    member = lax.axis_index("fsdp")
    shape = jax.ShapeDtypeStruct

    mixed = (gate_in.astype(jnp.float32) * values.astype(jnp.float32)).astype(jnp.bfloat16)
    mixed = lax.optimization_barrier(mixed)
    stage = exchange(mixed.reshape(devices, block, channels))

    held = []
    for shift in range(members):
        target = lax.rem(member + shift, members)
        piece = lax.dynamic_slice_in_dim(spectrum, target * channels, channels, 2)
        if shift > 0:
            ring = [(m, (m + shift) % members) for m in range(members)]
            piece = lax.ppermute(piece, "fsdp", ring)
        held.append(piece)

    cross = cross_table(devices, block, False, 1.0)
    cross_back = cross_table(devices, block, True, 2.0 / length)
    local = local_table(position, devices, rows, block, False)
    local_back = local_table(position, devices, rows, block, True)
    even, odd = filters(filter_tables(position, member, members, rows), held, rows, channels)

    spread = call(cross_kernel, (*cross, stage.reshape(rows, channels)), shape((2 * rows, channels), jnp.bfloat16), 12)
    stage = exchange(spread.reshape(devices, 2 * block, channels))
    wide = (devices, RADIX, 2 * block // RADIX, channels)
    turned = call(local_kernel, (*local, *local_back, even, odd, stage.reshape(wide)), shape(wide, jnp.bfloat16), 24)
    stage = exchange(turned.reshape(devices, 2 * block, channels))
    folded = call(
        cross_kernel, (*cross_back, stage.reshape(2 * rows, channels)), shape((rows, channels), jnp.bfloat16), 12
    )
    restored = exchange(folded.reshape(devices, block, channels)).reshape(rows, channels)
    convolved = restored.astype(jnp.float32) + bias[None, :] * mixed.astype(jnp.float32)
    return (gate_out.astype(jnp.float32) * convolved).astype(jnp.bfloat16)


def filters(tables, held, rows, channels):
    def whole(array):
        return pl.BlockSpec(array.shape, lambda i: (0, 0))

    def columns(*dims):
        return pl.BlockSpec((*dims, LANES), lambda i: (0,) * len(dims) + (i,))

    return pl.pallas_call(
        filter_kernel,
        grid=(channels // LANES,),
        in_specs=[whole(t) for t in tables] + [columns(*h.shape[:-1]) for h in held],
        out_specs=(columns(rows + 8), columns(rows)),
        out_shape=(
            jax.ShapeDtypeStruct((rows + 8, channels), jnp.float32),
            jax.ShapeDtypeStruct((rows, channels), jnp.float32),
        ),
        name="filters",
        compiler_params=pltpu.CompilerParams(vmem_limit_bytes=16 << 20),
    )(*tables, *held)


def solution(mesh):
    return jax.shard_map(
        body,
        mesh=mesh,
        in_specs=(
            P("ctx", "fsdp"),
            P("ctx", "fsdp"),
            P("ctx", "fsdp"),
            P("fsdp"),
            P(None, ("ctx", "fsdp"), None),
        ),
        out_specs=P("ctx", "fsdp"),
        check_vma=False,
    )
```

```python
import functools
import math

import jax
import jax.numpy as jnp
from jax import lax
from jax.experimental import pallas as pl
from jax.experimental.pallas import tpu as pltpu
from jax.sharding import PartitionSpec as P


LANES = 256
RADIX = 4
SPREAD = 1.624475


def cosine(step, modulus):
    half = modulus // 2
    centred = jnp.bitwise_and(step + half, modulus - 1) - half
    y = (modulus // 4 - jnp.abs(centred)).astype(jnp.float32) * (2.0 * math.pi / modulus)
    z = y * y
    series = 1.0 / 6227020800.0
    for term in (-1.0 / 39916800.0, 1.0 / 362880.0, -1.0 / 5040.0, 1.0 / 120.0, -1.0 / 6.0, 1.0):
        series = series * z + term
    return series * y


def split(table):
    high = lax.reduce_precision(table, 8, 7)
    return high.astype(jnp.bfloat16), (table - high).astype(jnp.bfloat16)


def message(index, block):
    fine = block // RADIX
    return index % fine * RADIX + index // (2 * fine) % RADIX, index // fine % 2


def cross_table(devices, block, transpose):
    wide = jnp.arange(2 * devices * block, dtype=jnp.int32)
    residue = wide // (2 * block)
    wide_row, part = message(wide, block)
    narrow = jnp.arange(devices * block, dtype=jnp.int32)
    place, narrow_row = narrow // block, narrow % block
    first = residue == 0
    rate = jnp.where(first, part * devices, residue)
    phase = jnp.where(first, 0, part * (devices // 2))
    if transpose:
        step = place[:, None] * rate[None, :] + phase[None, :]
        same = narrow_row[:, None] == wide_row[None, :]
    else:
        step = rate[:, None] * place[None, :] + phase[:, None]
        same = wide_row[:, None] == narrow_row[None, :]
    return jnp.where(same, cosine(step, 2 * devices) * SPREAD, 0.0).astype(jnp.bfloat16)


def local_table(position, devices, rows, block, transpose):
    length = 2 * devices * rows
    stride = 2 * devices
    fine = block // RADIX
    quart = rows // RADIX
    first = position == 0
    out = jnp.arange(4 * quart, dtype=jnp.int32)
    group, out_part, order = out // (2 * quart), out // quart % 2, out % quart
    rate = jnp.where(first, stride * order + group * devices, stride * (order + 2 * quart * group) + position)
    inp = jnp.arange(2 * devices * fine, dtype=jnp.int32)
    in_part = inp // fine % 2
    base = inp // (2 * fine) * block + inp % fine * RADIX
    in_phase = jnp.where(first, 0, in_part)
    side = jnp.where(first, group, 2)
    digit = jnp.arange(RADIX, dtype=jnp.int32)[:, None, None]
    quarter = length // 4
    if transpose:
        row = digit + base[None, :, None]
        step = row * rate[None, None, :] + quarter * (out_part[None, None, :] - in_phase[None, :, None])
        keep = (side[None, :] == 2) | (side[None, :] == in_part[:, None])
    else:
        row = digit + base[None, None, :]
        step = row * rate[None, :, None] + quarter * (out_part[None, :, None] - in_phase[None, None, :])
        keep = (side[:, None] == 2) | (side[:, None] == in_part[None, :])
    return split(jnp.where(keep[None], cosine(step, length), 0.0))


def filter_tables(position, member, members, rows):
    first = position == 0
    half = rows // 2
    out = jnp.arange(rows + 8, dtype=jnp.int32)
    order = jnp.minimum(out, rows - 1)
    upper = order >= half
    here = jnp.where(first, jnp.where(upper, rows + order - half, order), order)
    there = jnp.where(
        first,
        jnp.where(upper, 2 * rows - 1 - (order - half), (rows - order) % rows),
        2 * rows - 1 - order,
    )
    stored = jnp.arange(2 * rows, dtype=jnp.int32)
    part = 2 * rows // members
    stored = (member + members - stored // part) % members * part + stored % part
    hit_here = (stored[None, :] == here[:, None]).astype(jnp.float32)
    hit_there = (stored[None, :] == there[:, None]).astype(jnp.float32)
    weight = jnp.where(first & (order == 0), 0.25, 0.5)[:, None]
    even = weight * (hit_here + hit_there)
    odd = weight * (hit_here - hit_there)
    edge = jnp.where(first & (out[:, None] == rows) & (stored[None, :] == half), 0.5, 0.0)
    even = jnp.where((out < rows)[:, None], even, edge)
    return even.astype(jnp.bfloat16), odd[:rows].astype(jnp.bfloat16)


def dot(high, low, x):
    return jnp.dot(
        jnp.concatenate([high, low], axis=1),
        jnp.concatenate([x, x], axis=0),
        preferred_element_type=jnp.float32,
    )


def each_block(width, step):
    def go(i, carry):
        step(i, pl.ds(pl.multiple_of(i * LANES, LANES), LANES))
        return carry

    lax.fori_loop(0, width // LANES, go, 0)


def cross_kernel(scale, table_ref, x_ref, o_hbm, o_buf, o_sem):
    def store(i, cols):
        return pltpu.make_async_copy(o_buf.at[:, cols], o_hbm.at[:, cols], o_sem.at[i])

    def step(i, cols):
        acc = jnp.dot(table_ref[...], x_ref[:, cols], preferred_element_type=jnp.float32)
        o_buf[:, cols] = (acc * scale).astype(o_buf.dtype)
        store(i, cols).start()

    each_block(x_ref.shape[1], step)
    each_block(x_ref.shape[1], lambda i, cols: store(i, cols).wait())


def fold_kernel(scale, table_ref, x_ref, o_ref):
    def step(i, cols):
        acc = jnp.dot(table_ref[...], x_ref[:, cols], preferred_element_type=jnp.float32)
        o_ref[:, cols] = (acc * scale).astype(o_ref.dtype)

    each_block(x_ref.shape[1], step)


def filter_kernel(even_ref, odd_ref, *refs):
    *pieces, even_out, odd_out = refs
    rows = pieces[0].shape[1]
    even = odd = 0.0
    for shift, piece in enumerate(pieces):
        cols = slice(shift * rows, (shift + 1) * rows)
        even += jnp.dot(even_ref[:, cols], piece[0], preferred_element_type=jnp.float32)
        odd += jnp.dot(odd_ref[:, cols], piece[1], preferred_element_type=jnp.float32)
    even_out[...] = even
    odd_out[...] = odd


def local_kernel(
    mh_hbm, ml_hbm, gh_hbm, gl_hbm, even_hbm, odd_hbm, x_hbm, o_hbm,
    mh_ref, ml_ref, gh_ref, gl_ref, even_ref, odd_ref, x_ref, o_ref, m_sem, g_sem, h_sem, x_sem, o_sem,
):
    rows, width = odd_ref.shape
    quart = rows // RADIX

    def tables(sources, places, sems, digit):
        return [
            pltpu.make_async_copy(source.at[digit], place.at[digit], sems.at[n, digit])
            for n, (source, place) in enumerate(zip(sources, places))
        ]

    def forward(digit):
        return tables((mh_hbm, ml_hbm), (mh_ref, ml_ref), m_sem, digit) + [
            pltpu.make_async_copy(x_hbm.at[:, digit], x_ref.at[:, digit], x_sem.at[digit])
        ]

    def backward(digit):
        return tables((gh_hbm, gl_hbm), (gh_ref, gl_ref), g_sem, digit)

    def filters(i, cols):
        return [
            pltpu.make_async_copy(even_hbm.at[:, cols], even_ref.at[:, cols], h_sem.at[0, i]),
            pltpu.make_async_copy(odd_hbm.at[:, cols], odd_ref.at[:, cols], h_sem.at[1, i]),
        ]

    def store(i, cols):
        return pltpu.make_async_copy(o_ref.at[:, :, :, cols], o_hbm.at[:, :, :, cols], o_sem.at[i])

    def start(copies):
        for copy in copies:
            copy.start()

    def wait(copies):
        for copy in copies:
            copy.wait()

    for digit in range(RADIX):
        start(forward(digit))
    start(filters(0, pl.ds(0, LANES)))
    for digit in range(RADIX):
        start(backward(digit))
    for i in range(1, width // LANES):
        start(filters(i, pl.ds(i * LANES, LANES)))

    def step(i, cols):
        v = []
        for digit in range(RADIX):
            pl.when(i == 0)(lambda digit=digit: wait(forward(digit)))
            x = x_ref[:, digit, :, cols]
            v.append(dot(mh_ref[digit], ml_ref[digit], x.reshape(-1, x.shape[-1])))
        wait(filters(i, cols))
        sum02, sum13, gap02, gap13 = v[0] + v[2], v[1] + v[3], v[0] - v[2], v[1] - v[3]
        edge = (sum02[:8] - sum13[:8]) * even_ref[rows:, cols]
        total = sum02 + sum13
        packed = [[] for _ in range(RADIX)]
        for group in range(2):
            at = 2 * group * quart
            re, im = slice(at, at + quart), slice(at + quart, at + 2 * quart)
            parts = []
            for turn, (real, imag) in enumerate(
                ((total[re], total[im]), (gap02[re] + gap13[im], gap02[im] - gap13[re]))
            ):
                here = pl.ds(at + turn * quart, quart)
                even, odd = even_ref[here, cols], odd_ref[here, cols]
                parts.append((real * even - imag * odd, real * odd + imag * even))
            (r0, i0), (r1, i1) = parts
            for digit, (real, imag) in enumerate(
                ((r0 + r1, i0 + i1), (r0 - i1, i0 + r1), (r0 - r1, i0 - i1), (r0 + i1, i0 - r1))
            ):
                if group == 0:
                    top = real[:8] + edge if digit % 2 == 0 else real[:8] - edge
                    packed[digit].append(jnp.concatenate([top, real[8:]], axis=0))
                else:
                    packed[digit].append(real)
                packed[digit].append(imag)
        for digit in range(RADIX):
            pl.when(i == 0)(lambda digit=digit: wait(backward(digit)))
            b = jnp.concatenate(packed[digit], axis=0).astype(jnp.bfloat16)
            y = dot(gh_ref[digit], gl_ref[digit], b)
            o_ref[:, digit, :, cols] = y.reshape(o_ref.shape[0], o_ref.shape[2], -1).astype(o_ref.dtype)
        store(i, cols).start()

    each_block(width, step)
    each_block(width, lambda i, cols: store(i, cols).wait())


def gate_kernel(restored_ref, mixed_ref, gate_ref, bias_ref, o_hbm, o_buf, o_sem):
    rows = o_buf.shape[0] // o_sem.shape[0]
    bias = bias_ref[...]

    def store(i):
        at = pl.ds(i * rows, rows)
        return pltpu.make_async_copy(o_buf.at[at], o_hbm.at[at], o_sem.at[i])

    for i in range(o_sem.shape[0]):
        at = slice(i * rows, (i + 1) * rows)
        convolved = restored_ref[at].astype(jnp.float32) + bias * mixed_ref[at].astype(jnp.float32)
        o_buf[at] = (gate_ref[at].astype(jnp.float32) * convolved).astype(o_buf.dtype)
        store(i).start()
    for i in range(o_sem.shape[0]):
        store(i).wait()


def call(kernel, stored, near, out, scratch, grant):
    there = pl.BlockSpec(memory_space=pltpu.HBM)
    return pl.pallas_call(
        kernel,
        in_specs=[there] * len(stored) + [pl.BlockSpec(memory_space=pltpu.VMEM)] * len(near),
        out_specs=there,
        out_shape=out,
        scratch_shapes=scratch,
        compiler_params=pltpu.CompilerParams(vmem_limit_bytes=grant << 20),
    )(*stored, *near)


def apply_cross(table, x, scale):
    out = jax.ShapeDtypeStruct((table.shape[0], x.shape[1]), jnp.bfloat16)
    scratch = [pltpu.VMEM(out.shape, out.dtype), pltpu.SemaphoreType.DMA((x.shape[1] // LANES,))]
    return call(functools.partial(cross_kernel, scale), (), (table, x), out, scratch, 12)


def apply_fold(table, x, scale):
    vmem = pl.BlockSpec(memory_space=pltpu.VMEM)
    return pl.pallas_call(
        functools.partial(fold_kernel, scale),
        in_specs=[vmem] * 2,
        out_specs=vmem,
        out_shape=jax.ShapeDtypeStruct((table.shape[0], x.shape[1]), jnp.bfloat16),
        name="fold",
        compiler_params=pltpu.CompilerParams(vmem_limit_bytes=12 << 20),
    )(table, x)


def apply_local(tables, even, odd, x):
    count = x.shape[-1] // LANES
    dma = pltpu.SemaphoreType.DMA
    scratch = [pltpu.VMEM(t.shape, t.dtype) for t in (*tables, even, odd, x, x)]
    scratch += [dma((2, RADIX)), dma((2, RADIX)), dma((2, count)), dma((RADIX,)), dma((count,))]
    out = jax.ShapeDtypeStruct(x.shape, x.dtype)
    return call(local_kernel, (*tables, even, odd, x), (), out, scratch, 62)


def apply_gate(restored, mixed, gate_out, bias):
    scratch = [pltpu.VMEM(mixed.shape, mixed.dtype), pltpu.SemaphoreType.DMA((4,))]
    out = jax.ShapeDtypeStruct(mixed.shape, mixed.dtype)
    return call(gate_kernel, (), (restored, mixed, gate_out, bias[None, :]), out, scratch, 8)


def exchange(array):
    return lax.all_to_all(array, "ctx", split_axis=0, concat_axis=0, tiled=True)


def body(gate_in, values, gate_out, bias, spectrum):
    devices = lax.axis_size("ctx")
    members = lax.axis_size("fsdp")
    rows, channels = gate_in.shape
    block = rows // devices
    length = 2 * rows * devices
    position = lax.axis_index("ctx")
    member = lax.axis_index("fsdp")

    def piece_for(stored, shift):
        target = lax.rem(member + shift, members)
        return lax.dynamic_slice_in_dim(stored, target * channels, channels, 2)

    def send(piece, shift):
        return lax.ppermute(piece, "fsdp", [(m, (m + shift) % members) for m in range(members)])

    far = members // 2
    held = {}
    ahead = piece_for(spectrum, far)
    held[far] = send(ahead, far)
    mixed = (gate_in.astype(jnp.float32) * values.astype(jnp.float32)).astype(jnp.bfloat16)
    mixed, later = lax.optimization_barrier((mixed, spectrum))
    stage = exchange(mixed.reshape(devices, block, channels))
    for shift in (1, members - 1, 0):
        piece = piece_for(later, shift)
        held[shift] = send(piece, shift) if shift else piece
    held = [held[shift] for shift in range(members)]

    cross = cross_table(devices, block, False)
    cross_back = cross_table(devices, block, True)
    local = local_table(position, devices, rows, block, False)
    local_back = local_table(position, devices, rows, block, True)
    even, odd = filters(filter_tables(position, member, members, rows), held, rows, channels)

    spread = apply_cross(cross, stage.reshape(rows, channels), 1.0 / SPREAD)
    stage = exchange(spread.reshape(devices, 2 * block, channels))
    turned = apply_local(local + local_back, even, odd, stage.reshape(devices, RADIX, -1, channels))
    stage = exchange(turned.reshape(devices, 2 * block, channels))
    folded = apply_fold(cross_back, stage.reshape(2 * rows, channels), 2.0 / (length * SPREAD))
    restored = exchange(folded.reshape(devices, block, channels)).reshape(rows, channels)
    return apply_gate(restored, mixed, gate_out, bias)


def filters(tables, held, rows, channels):
    def whole(array):
        return pl.BlockSpec(array.shape, lambda i: (0, 0))

    def columns(*dims):
        return pl.BlockSpec((*dims, LANES), lambda i: (0,) * len(dims) + (i,))

    return pl.pallas_call(
        filter_kernel,
        grid=(channels // LANES,),
        in_specs=[whole(t) for t in tables] + [columns(*h.shape[:-1]) for h in held],
        out_specs=(columns(rows + 8), columns(rows)),
        out_shape=(
            jax.ShapeDtypeStruct((rows + 8, channels), jnp.float32),
            jax.ShapeDtypeStruct((rows, channels), jnp.float32),
        ),
        name="filters",
        compiler_params=pltpu.CompilerParams(vmem_limit_bytes=62 << 20),
    )(*tables, *held)


def solution(mesh):
    return jax.shard_map(
        body,
        mesh=mesh,
        in_specs=(
            P("ctx", "fsdp"),
            P("ctx", "fsdp"),
            P("ctx", "fsdp"),
            P("fsdp"),
            P(None, ("ctx", "fsdp"), None),
        ),
        out_specs=P("ctx", "fsdp"),
        check_vma=False,
    )
```

```python
import functools
import math

import jax
import jax.numpy as jnp
from jax import lax
from jax.experimental import pallas as pl
from jax.experimental.pallas import tpu as pltpu
from jax.sharding import PartitionSpec as P


LANES = 512
RADIX = 4
SPREAD = 1.624475


def cosine(step, modulus):
    half = modulus // 2
    centred = jnp.bitwise_and(step + half, modulus - 1) - half
    y = (modulus // 4 - jnp.abs(centred)).astype(jnp.float32) * (2.0 * math.pi / modulus)
    z = y * y
    series = 1.0 / 6227020800.0
    for term in (-1.0 / 39916800.0, 1.0 / 362880.0, -1.0 / 5040.0, 1.0 / 120.0, -1.0 / 6.0, 1.0):
        series = series * z + term
    return series * y


def message(index, block):
    fine = block // RADIX
    return index % fine * RADIX + index // (2 * fine) % RADIX, index // fine % 2


def cross_table(devices, block, transpose):
    wide = jnp.arange(2 * devices * block, dtype=jnp.int32)
    residue = wide // (2 * block)
    wide_row, part = message(wide, block)
    narrow = jnp.arange(devices * block, dtype=jnp.int32)
    place, narrow_row = narrow // block, narrow % block
    first = residue == 0
    rate = jnp.where(first, part * devices, residue)
    phase = jnp.where(first, 0, part * (devices // 2))
    if transpose:
        step = place[:, None] * rate[None, :] + phase[None, :]
        same = narrow_row[:, None] == wide_row[None, :]
    else:
        step = rate[:, None] * place[None, :] + phase[:, None]
        same = wide_row[:, None] == narrow_row[None, :]
    return jnp.where(same, cosine(step, 2 * devices) * SPREAD, 0.0).astype(jnp.bfloat16)


def local_table(position, devices, rows, block, transpose):
    length = 2 * devices * rows
    stride = 2 * devices
    fine = block // RADIX
    quart = rows // RADIX
    first = position == 0
    out = jnp.arange(4 * quart, dtype=jnp.int32)
    group, out_part, order = out // (2 * quart), out // quart % 2, out % quart
    rate = jnp.where(first, stride * order + group * devices, stride * (order + 2 * quart * group) + position)
    inp = jnp.arange(2 * devices * fine, dtype=jnp.int32)
    in_part = inp // fine % 2
    base = inp // (2 * fine) * block + inp % fine * RADIX
    in_phase = jnp.where(first, 0, in_part)
    side = jnp.where(first, group, 2)
    digit = jnp.arange(RADIX, dtype=jnp.int32)[:, None, None]
    quarter = length // 4
    if transpose:
        row = digit + base[None, :, None]
        step = row * rate[None, None, :] + quarter * (out_part[None, None, :] - in_phase[None, :, None])
        keep = (side[None, :] == 2) | (side[None, :] == in_part[:, None])
    else:
        row = digit + base[None, None, :]
        step = row * rate[None, :, None] + quarter * (out_part[None, :, None] - in_phase[None, None, :])
        keep = (side[:, None] == 2) | (side[:, None] == in_part[None, :])
    return jnp.where(keep[None], cosine(step, length), 0.0).astype(jnp.bfloat16)


def filter_tables(position, member, members, rows):
    first = position == 0
    half = rows // 2
    out = jnp.arange(rows + 8, dtype=jnp.int32)
    order = jnp.minimum(out, rows - 1)
    upper = order >= half
    here = jnp.where(first, jnp.where(upper, rows + order - half, order), order)
    there = jnp.where(
        first,
        jnp.where(upper, 2 * rows - 1 - (order - half), (rows - order) % rows),
        2 * rows - 1 - order,
    )
    stored = jnp.arange(2 * rows, dtype=jnp.int32)
    part = 2 * rows // members
    stored = (member + members - stored // part) % members * part + stored % part
    hit_here = (stored[None, :] == here[:, None]).astype(jnp.float32)
    hit_there = (stored[None, :] == there[:, None]).astype(jnp.float32)
    weight = jnp.where(first & (order == 0), 0.25, 0.5)[:, None]
    even = weight * (hit_here + hit_there)
    odd = weight * (hit_here - hit_there)
    edge = jnp.where(first & (out[:, None] == rows) & (stored[None, :] == half), 0.5, 0.0)
    even = jnp.where((out < rows)[:, None], even, edge)
    return even.astype(jnp.bfloat16), odd[:rows].astype(jnp.bfloat16)


def each_block(width, step):
    def go(i, carry):
        step(i, pl.ds(pl.multiple_of(i * LANES, LANES), LANES))
        return carry

    lax.fori_loop(0, width // LANES, go, 0)


def cross_kernel(scale, table_ref, x_ref, o_hbm, o_buf, o_sem):
    def store(i, cols):
        return pltpu.make_async_copy(o_buf.at[:, cols], o_hbm.at[:, cols], o_sem.at[i])

    def step(i, cols):
        acc = jnp.dot(table_ref[...], x_ref[:, cols], preferred_element_type=jnp.float32)
        o_buf[:, cols] = (acc * scale).astype(o_buf.dtype)
        store(i, cols).start()

    each_block(x_ref.shape[1], step)
    each_block(x_ref.shape[1], lambda i, cols: store(i, cols).wait())


def fold_kernel(scale, table_ref, x_ref, o_ref):
    def step(i, cols):
        acc = jnp.dot(table_ref[...], x_ref[:, cols], preferred_element_type=jnp.float32)
        o_ref[:, cols] = (acc * scale).astype(o_ref.dtype)

    each_block(x_ref.shape[1], step)


def filter_kernel(even_ref, odd_ref, *refs):
    *pieces, even_out, odd_out = refs
    rows = pieces[0].shape[1]
    even = odd = 0.0
    for shift, piece in enumerate(pieces):
        cols = slice(shift * rows, (shift + 1) * rows)
        even += jnp.dot(even_ref[:, cols], piece[0], preferred_element_type=jnp.float32)
        odd += jnp.dot(odd_ref[:, cols], piece[1], preferred_element_type=jnp.float32)
    even_out[...] = even
    odd_out[...] = odd


def local_kernel(
    m_hbm, g_hbm, even_hbm, odd_hbm, x_hbm, o_hbm,
    m_ref, g_ref, even_ref, odd_ref, x_ref, o_ref, b_ref, m_sem, g_sem, h_sem, x_sem, o_sem,
):
    rows, width = odd_ref.shape
    quart = rows // RADIX

    forward = pltpu.make_async_copy(m_hbm, m_ref, m_sem)
    backward = pltpu.make_async_copy(g_hbm, g_ref, g_sem)

    def incoming(i, cols):
        return pltpu.make_async_copy(x_hbm.at[:, :, :, cols], x_ref.at[:, :, :, cols], x_sem.at[i])

    def filters(i, cols):
        return [
            pltpu.make_async_copy(even_hbm.at[:, cols], even_ref.at[:, cols], h_sem.at[0, i]),
            pltpu.make_async_copy(odd_hbm.at[:, cols], odd_ref.at[:, cols], h_sem.at[1, i]),
        ]

    def store(i, cols):
        return pltpu.make_async_copy(o_ref.at[:, :, :, cols], o_hbm.at[:, :, :, cols], o_sem.at[i])

    def start(copies):
        for copy in copies:
            copy.start()

    def wait(copies):
        for copy in copies:
            copy.wait()

    forward.start()
    for i in range(width // LANES):
        incoming(i, pl.ds(i * LANES, LANES)).start()
        start(filters(i, pl.ds(i * LANES, LANES)))
    backward.start()
    forward.wait()

    def ahead(i, cols):
        incoming(i, cols).wait()
        v = []
        for digit in range(RADIX):
            x = x_ref[:, digit, :, cols]
            x = x.reshape(-1, x.shape[-1])
            v.append(jnp.dot(m_ref[digit], x, preferred_element_type=jnp.float32))
        wait(filters(i, cols))
        sum02, sum13, gap02, gap13 = v[0] + v[2], v[1] + v[3], v[0] - v[2], v[1] - v[3]
        edge = (sum02[:8] - sum13[:8]) * even_ref[rows:, cols]
        total = sum02 + sum13
        for group in range(2):
            at = 2 * group * quart
            re, im = slice(at, at + quart), slice(at + quart, at + 2 * quart)
            parts = []
            for turn, (real, imag) in enumerate(
                ((total[re], total[im]), (gap02[re] + gap13[im], gap02[im] - gap13[re]))
            ):
                here = pl.ds(at + turn * quart, quart)
                even, odd = even_ref[here, cols], odd_ref[here, cols]
                parts.append((real * even - imag * odd, real * odd + imag * even))
            (r0, i0), (r1, i1) = parts
            for digit, (real, imag) in enumerate(
                ((r0 + r1, i0 + i1), (r0 - i1, i0 + r1), (r0 - r1, i0 - i1), (r0 + i1, i0 - r1))
            ):
                if group == 0:
                    top = real[:8] + edge if digit % 2 == 0 else real[:8] - edge
                    real = jnp.concatenate([top, real[8:]], axis=0)
                b_ref[digit, re, cols] = real.astype(b_ref.dtype)
                b_ref[digit, im, cols] = imag.astype(b_ref.dtype)

    def back(i, cols):
        for digit in range(RADIX):
            y = jnp.dot(g_ref[digit], b_ref[digit, :, cols], preferred_element_type=jnp.float32)
            o_ref[:, digit, :, cols] = y.reshape(o_ref.shape[0], o_ref.shape[2], -1).astype(o_ref.dtype)
        store(i, cols).start()

    each_block(width, ahead)
    backward.wait()
    each_block(width, back)
    each_block(width, lambda i, cols: store(i, cols).wait())


def gate_kernel(restored_ref, mixed_ref, gate_ref, bias_ref, o_hbm, o_buf, o_sem):
    rows = o_buf.shape[0] // o_sem.shape[0]
    bias = bias_ref[...]

    def store(i):
        at = pl.ds(i * rows, rows)
        return pltpu.make_async_copy(o_buf.at[at], o_hbm.at[at], o_sem.at[i])

    for i in range(o_sem.shape[0]):
        at = slice(i * rows, (i + 1) * rows)
        convolved = restored_ref[at].astype(jnp.float32) + bias * mixed_ref[at].astype(jnp.float32)
        o_buf[at] = (gate_ref[at].astype(jnp.float32) * convolved).astype(o_buf.dtype)
        store(i).start()
    for i in range(o_sem.shape[0]):
        store(i).wait()


def call(kernel, stored, near, out, scratch, grant):
    there = pl.BlockSpec(memory_space=pltpu.HBM)
    return pl.pallas_call(
        kernel,
        in_specs=[there] * len(stored) + [pl.BlockSpec(memory_space=pltpu.VMEM)] * len(near),
        out_specs=there,
        out_shape=out,
        scratch_shapes=scratch,
        compiler_params=pltpu.CompilerParams(vmem_limit_bytes=grant << 20),
    )(*stored, *near)


def apply_cross(table, x, scale):
    out = jax.ShapeDtypeStruct((table.shape[0], x.shape[1]), jnp.bfloat16)
    scratch = [pltpu.VMEM(out.shape, out.dtype), pltpu.SemaphoreType.DMA((x.shape[1] // LANES,))]
    return call(functools.partial(cross_kernel, scale), (), (table, x), out, scratch, 12)


def apply_fold(table, x, scale):
    vmem = pl.BlockSpec(memory_space=pltpu.VMEM)
    return pl.pallas_call(
        functools.partial(fold_kernel, scale),
        in_specs=[vmem] * 2,
        out_specs=vmem,
        out_shape=jax.ShapeDtypeStruct((table.shape[0], x.shape[1]), jnp.bfloat16),
        name="fold",
        compiler_params=pltpu.CompilerParams(vmem_limit_bytes=12 << 20),
    )(table, x)


def apply_local(forward, backward, even, odd, x):
    count = x.shape[-1] // LANES
    dma = pltpu.SemaphoreType.DMA
    scratch = [pltpu.VMEM(t.shape, t.dtype) for t in (forward, backward, even, odd, x, x)]
    scratch += [pltpu.VMEM((RADIX, odd.shape[0], odd.shape[1]), x.dtype)]
    scratch += [dma(()), dma(()), dma((2, count)), dma((count,)), dma((count,))]
    out = jax.ShapeDtypeStruct(x.shape, x.dtype)
    return call(local_kernel, (forward, backward, even, odd, x), (), out, scratch, 62)


def apply_gate(restored, mixed, gate_out, bias):
    scratch = [pltpu.VMEM(mixed.shape, mixed.dtype), pltpu.SemaphoreType.DMA((4,))]
    out = jax.ShapeDtypeStruct(mixed.shape, mixed.dtype)
    return call(gate_kernel, (), (restored, mixed, gate_out, bias[None, :]), out, scratch, 8)


def exchange(array):
    return lax.all_to_all(array, "ctx", split_axis=0, concat_axis=0, tiled=True)


def body(gate_in, values, gate_out, bias, spectrum):
    devices = lax.axis_size("ctx")
    members = lax.axis_size("fsdp")
    rows, channels = gate_in.shape
    block = rows // devices
    length = 2 * rows * devices
    position = lax.axis_index("ctx")
    member = lax.axis_index("fsdp")

    def piece_for(stored, shift):
        target = lax.rem(member + shift, members)
        return lax.dynamic_slice_in_dim(stored, target * channels, channels, 2)

    def send(piece, shift):
        return lax.ppermute(piece, "fsdp", [(m, (m + shift) % members) for m in range(members)])

    far = members // 2
    held = {}
    ahead = piece_for(spectrum, far)
    held[far] = send(ahead, far)
    mixed = (gate_in.astype(jnp.float32) * values.astype(jnp.float32)).astype(jnp.bfloat16)
    mixed, later = lax.optimization_barrier((mixed, spectrum))
    stage = exchange(mixed.reshape(devices, block, channels))
    for shift in (1, members - 1, 0):
        piece = piece_for(later, shift)
        held[shift] = send(piece, shift) if shift else piece
    held = [held[shift] for shift in range(members)]

    cross = cross_table(devices, block, False)
    cross_back = cross_table(devices, block, True)
    local = local_table(position, devices, rows, block, False)
    local_back = local_table(position, devices, rows, block, True)
    even, odd = filters(filter_tables(position, member, members, rows), held, rows, channels)

    spread = apply_cross(cross, stage.reshape(rows, channels), 1.0 / SPREAD)
    stage = exchange(spread.reshape(devices, 2 * block, channels))
    turned = apply_local(local, local_back, even, odd, stage.reshape(devices, RADIX, -1, channels))
    stage = exchange(turned.reshape(devices, 2 * block, channels))
    folded = apply_fold(cross_back, stage.reshape(2 * rows, channels), 2.0 / (length * SPREAD))
    restored = exchange(folded.reshape(devices, block, channels)).reshape(rows, channels)
    return apply_gate(restored, mixed, gate_out, bias)


def filters(tables, held, rows, channels):
    def whole(array):
        return pl.BlockSpec(array.shape, lambda i: (0, 0))

    def columns(*dims):
        return pl.BlockSpec((*dims, LANES), lambda i: (0,) * len(dims) + (i,))

    return pl.pallas_call(
        filter_kernel,
        grid=(channels // LANES,),
        in_specs=[whole(t) for t in tables] + [columns(*h.shape[:-1]) for h in held],
        out_specs=(columns(rows + 8), columns(rows)),
        out_shape=(
            jax.ShapeDtypeStruct((rows + 8, channels), jnp.float32),
            jax.ShapeDtypeStruct((rows, channels), jnp.float32),
        ),
        name="filters",
        compiler_params=pltpu.CompilerParams(vmem_limit_bytes=62 << 20),
    )(*tables, *held)


def solution(mesh):
    return jax.shard_map(
        body,
        mesh=mesh,
        in_specs=(
            P("ctx", "fsdp"),
            P("ctx", "fsdp"),
            P("ctx", "fsdp"),
            P("fsdp"),
            P(None, ("ctx", "fsdp"), None),
        ),
        out_specs=P("ctx", "fsdp"),
        check_vma=False,
    )
```

```python
import functools
import math

import jax
import jax.numpy as jnp
from jax import lax
from jax.experimental import pallas as pl
from jax.experimental.pallas import tpu as pltpu
from jax.sharding import PartitionSpec as P


LANES = 512
RADIX = 4
SPREAD = 1.624475


def cosine(step, modulus):
    half = modulus // 2
    centred = jnp.bitwise_and(step + half, modulus - 1) - half
    y = (modulus // 4 - jnp.abs(centred)).astype(jnp.float32) * (2.0 * math.pi / modulus)
    z = y * y
    series = 1.0 / 6227020800.0
    for term in (-1.0 / 39916800.0, 1.0 / 362880.0, -1.0 / 5040.0, 1.0 / 120.0, -1.0 / 6.0, 1.0):
        series = series * z + term
    return series * y


def message(index, block):
    fine = block // RADIX
    return index % fine * RADIX + index // (2 * fine) % RADIX, index // fine % 2


def cross_table(devices, block, transpose):
    wide = jnp.arange(2 * devices * block, dtype=jnp.int32)
    residue = wide // (2 * block)
    wide_row, part = message(wide, block)
    narrow = jnp.arange(devices * block, dtype=jnp.int32)
    place, narrow_row = narrow // block, narrow % block
    first = residue == 0
    rate = jnp.where(first, part * devices, residue)
    phase = jnp.where(first, 0, part * (devices // 2))
    if transpose:
        step = place[:, None] * rate[None, :] + phase[None, :]
        same = narrow_row[:, None] == wide_row[None, :]
    else:
        step = rate[:, None] * place[None, :] + phase[:, None]
        same = wide_row[:, None] == narrow_row[None, :]
    return jnp.where(same, cosine(step, 2 * devices) * SPREAD, 0.0).astype(jnp.bfloat16)


def local_table(position, devices, rows, block, transpose):
    length = 2 * devices * rows
    stride = 2 * devices
    fine = block // RADIX
    quart = rows // RADIX
    first = position == 0
    out = jnp.arange(4 * quart, dtype=jnp.int32)
    group, out_part, order = out // (2 * quart), out // quart % 2, out % quart
    rate = jnp.where(first, stride * order + group * devices, stride * (order + 2 * quart * group) + position)
    inp = jnp.arange(2 * devices * fine, dtype=jnp.int32)
    in_part = inp // fine % 2
    base = inp // (2 * fine) * block + inp % fine * RADIX
    in_phase = jnp.where(first, 0, in_part)
    side = jnp.where(first, group, 2)
    digit = jnp.arange(RADIX, dtype=jnp.int32)[:, None, None]
    quarter = length // 4
    if transpose:
        row = digit + base[None, :, None]
        step = row * rate[None, None, :] + quarter * (out_part[None, None, :] - in_phase[None, :, None])
        keep = (side[None, :] == 2) | (side[None, :] == in_part[:, None])
    else:
        row = digit + base[None, None, :]
        step = row * rate[None, :, None] + quarter * (out_part[None, :, None] - in_phase[None, None, :])
        keep = (side[:, None] == 2) | (side[:, None] == in_part[None, :])
    return jnp.where(keep[None], cosine(step, length), 0.0).astype(jnp.bfloat16)


def each_block(width, step):
    def go(i, carry):
        step(i, pl.ds(pl.multiple_of(i * LANES, LANES), LANES))
        return carry

    lax.fori_loop(0, width // LANES, go, 0)


def cross_kernel(scale, table_ref, x_ref, o_hbm, o_buf, o_sem):
    def store(i, cols):
        return pltpu.make_async_copy(o_buf.at[:, cols], o_hbm.at[:, cols], o_sem.at[i])

    def step(i, cols):
        acc = jnp.dot(table_ref[...], x_ref[:, cols], preferred_element_type=jnp.float32)
        o_buf[:, cols] = (acc * scale).astype(o_buf.dtype)
        store(i, cols).start()

    each_block(x_ref.shape[1], step)
    each_block(x_ref.shape[1], lambda i, cols: store(i, cols).wait())


def fold_kernel(scale, table_ref, x_ref, o_ref):
    def step(i, cols):
        acc = jnp.dot(table_ref[...], x_ref[:, cols], preferred_element_type=jnp.float32)
        o_ref[:, cols] = (acc * scale).astype(o_ref.dtype)

    each_block(x_ref.shape[1], step)


def local_kernel(
    m_hbm, g_hbm, own_hbm, near_hbm, far_hbm, last_hbm, x_hbm, o_hbm,
    m_ref, g_ref, r_ref, x_ref, o_ref, b_ref, m_sem, g_sem, r_sem, x_sem, o_sem,
):
    quart, width = r_ref.shape[2] // 2, r_ref.shape[3]
    first = lax.axis_index("ctx") == 0
    member = lax.axis_index("fsdp")
    members = r_ref.shape[0]

    forward = pltpu.make_async_copy(m_hbm, m_ref, m_sem)
    backward = pltpu.make_async_copy(g_hbm, g_ref, g_sem)

    def filters(i, cols):
        mine = pl.ds(pl.multiple_of(member * width + i * LANES, LANES), LANES)
        sources = [own_hbm.at[:, :, mine]] + [piece.at[:, :, cols] for piece in (near_hbm, far_hbm, last_hbm)]
        return [
            pltpu.make_async_copy(source, r_ref.at[shift, :, :, cols], r_sem.at[shift, i])
            for shift, source in enumerate(sources)
        ]

    def response(group, cols):
        here = jnp.where(first, 2 * group, group)
        there = jnp.where(first, 2 * group + 1, members - 1 - group)
        here = lax.rem(member + members - here, members)
        there = lax.rem(member + members - there, members)
        size = 2 * quart
        row = lax.broadcasted_iota(jnp.int32, (size, size), 0)
        col = lax.broadcasted_iota(jnp.int32, (size, size), 1)
        shifted = jnp.where(first, 1, 0) if group == 0 else 0
        mirror = jnp.where(row + col == size - 1 + shifted, 0.5, 0.0).astype(jnp.bfloat16)
        even = 0.5 * r_ref[here, 0, :, cols].astype(jnp.float32) + jnp.dot(
            mirror, r_ref[there, 0, :, cols], preferred_element_type=jnp.float32
        )
        odd = 0.5 * r_ref[here, 1, :, cols].astype(jnp.float32) - jnp.dot(
            mirror, r_ref[there, 1, :, cols], preferred_element_type=jnp.float32
        )
        return even, odd, there

    def incoming(i, cols):
        return pltpu.make_async_copy(x_hbm.at[:, :, :, cols], x_ref.at[:, :, :, cols], x_sem.at[i])

    def store(i, cols):
        return pltpu.make_async_copy(o_ref.at[:, :, :, cols], o_hbm.at[:, :, :, cols], o_sem.at[i])

    def start(copies):
        for copy in copies:
            copy.start()

    def wait(copies):
        for copy in copies:
            copy.wait()

    forward.start()
    for i in range(width // LANES):
        incoming(i, pl.ds(i * LANES, LANES)).start()
        start(filters(i, pl.ds(i * LANES, LANES)))
    backward.start()
    forward.wait()

    def ahead(i, cols):
        incoming(i, cols).wait()
        v = []
        for digit in range(RADIX):
            x = x_ref[:, digit, :, cols]
            x = x.reshape(-1, x.shape[-1])
            v.append(jnp.dot(m_ref[digit], x, preferred_element_type=jnp.float32))
        wait(filters(i, cols))
        sum02, sum13, gap02, gap13 = v[0] + v[2], v[1] + v[3], v[0] - v[2], v[1] - v[3]
        total = sum02 + sum13
        for group in range(2):
            even, odd, there = response(group, cols)
            if group == 0:
                lone = first & (lax.broadcasted_iota(jnp.int32, (8, LANES), 0) == 0)
                edge = jnp.where(lone, 0.5 * r_ref[there, 0, :8, cols].astype(jnp.float32), 0.0)
                edge = (sum02[:8] - sum13[:8]) * edge
            at = 2 * group * quart
            re, im = slice(at, at + quart), slice(at + quart, at + 2 * quart)
            parts = []
            for turn, (real, imag) in enumerate(
                ((total[re], total[im]), (gap02[re] + gap13[im], gap02[im] - gap13[re]))
            ):
                here = slice(turn * quart, (turn + 1) * quart)
                parts.append((real * even[here] - imag * odd[here], real * odd[here] + imag * even[here]))
            (r0, i0), (r1, i1) = parts
            for digit, (real, imag) in enumerate(
                ((r0 + r1, i0 + i1), (r0 - i1, i0 + r1), (r0 - r1, i0 - i1), (r0 + i1, i0 - r1))
            ):
                if group == 0:
                    top = real[:8] + edge if digit % 2 == 0 else real[:8] - edge
                    real = jnp.concatenate([top, real[8:]], axis=0)
                b_ref[digit, re, cols] = real.astype(b_ref.dtype)
                b_ref[digit, im, cols] = imag.astype(b_ref.dtype)

    def back(i, cols):
        for digit in range(RADIX):
            y = jnp.dot(g_ref[digit], b_ref[digit, :, cols], preferred_element_type=jnp.float32)
            o_ref[:, digit, :, cols] = y.reshape(o_ref.shape[0], o_ref.shape[2], -1).astype(o_ref.dtype)
        store(i, cols).start()

    each_block(width, ahead)
    backward.wait()
    each_block(width, back)
    each_block(width, lambda i, cols: store(i, cols).wait())


def gate_kernel(restored_ref, mixed_ref, gate_ref, bias_ref, o_hbm, o_buf, o_sem):
    rows = o_buf.shape[0] // o_sem.shape[0]
    bias = bias_ref[...]

    def store(i):
        at = pl.ds(i * rows, rows)
        return pltpu.make_async_copy(o_buf.at[at], o_hbm.at[at], o_sem.at[i])

    for i in range(o_sem.shape[0]):
        at = slice(i * rows, (i + 1) * rows)
        convolved = restored_ref[at].astype(jnp.float32) + bias * mixed_ref[at].astype(jnp.float32)
        o_buf[at] = (gate_ref[at].astype(jnp.float32) * convolved).astype(o_buf.dtype)
        store(i).start()
    for i in range(o_sem.shape[0]):
        store(i).wait()


def call(kernel, stored, near, out, scratch, grant):
    there = pl.BlockSpec(memory_space=pltpu.HBM)
    return pl.pallas_call(
        kernel,
        in_specs=[there] * len(stored) + [pl.BlockSpec(memory_space=pltpu.VMEM)] * len(near),
        out_specs=jax.tree.map(lambda _: there, out),
        out_shape=out,
        scratch_shapes=scratch,
        compiler_params=pltpu.CompilerParams(vmem_limit_bytes=grant << 20),
    )(*stored, *near)


def apply_cross(table, x, scale):
    out = jax.ShapeDtypeStruct((table.shape[0], x.shape[1]), jnp.bfloat16)
    scratch = [pltpu.VMEM(out.shape, out.dtype), pltpu.SemaphoreType.DMA((x.shape[1] // LANES,))]
    return call(functools.partial(cross_kernel, scale), (), (table, x), out, scratch, 12)


def apply_fold(table, x, scale):
    vmem = pl.BlockSpec(memory_space=pltpu.VMEM)
    return pl.pallas_call(
        functools.partial(fold_kernel, scale),
        in_specs=[vmem] * 2,
        out_specs=vmem,
        out_shape=jax.ShapeDtypeStruct((table.shape[0], x.shape[1]), jnp.bfloat16),
        name="fold",
        compiler_params=pltpu.CompilerParams(vmem_limit_bytes=12 << 20),
    )(table, x)


def apply_local(forward, backward, pieces, x):
    count = x.shape[-1] // LANES
    rows = forward.shape[1]
    dma = pltpu.SemaphoreType.DMA
    stored = pltpu.VMEM((len(pieces), *pieces[1].shape), x.dtype)
    scratch = [pltpu.VMEM(forward.shape, x.dtype), pltpu.VMEM(backward.shape, x.dtype), stored]
    scratch += [pltpu.VMEM(x.shape, x.dtype), pltpu.VMEM(x.shape, x.dtype)]
    scratch += [pltpu.VMEM((RADIX, rows, x.shape[-1]), x.dtype)]
    scratch += [dma(()), dma(()), dma((len(pieces), count)), dma((count,)), dma((count,))]
    out = jax.ShapeDtypeStruct(x.shape, x.dtype)
    return call(local_kernel, (forward, backward, *pieces, x), (), out, scratch, 62)


def mix_kernel(left_hbm, right_hbm, stored_hbm, o_hbm, far_hbm, left, right, o_buf, in_sem, far_sem, o_sem):
    blocks = o_sem.shape[0]
    rows = o_buf.shape[0] // blocks
    width = far_hbm.shape[2]
    target = lax.rem(lax.axis_index("fsdp") + 2, stored_hbm.shape[2] // width)

    def loads(i):
        at = pl.ds(i * rows, rows)
        return [
            pltpu.make_async_copy(left_hbm.at[at], left.at[at], in_sem.at[0, i]),
            pltpu.make_async_copy(right_hbm.at[at], right.at[at], in_sem.at[1, i]),
        ]

    def store(i):
        at = pl.ds(i * rows, rows)
        return pltpu.make_async_copy(o_buf.at[at], o_hbm.at[at], o_sem.at[i])

    for i in range(blocks):
        for load in loads(i):
            load.start()
    mine = pl.ds(pl.multiple_of(target * width, width), width)
    far = pltpu.make_async_copy(stored_hbm.at[:, :, mine], far_hbm, far_sem)
    far.start()
    for i in range(blocks):
        for load in loads(i):
            load.wait()
        at = slice(i * rows, (i + 1) * rows)
        o_buf[at] = (left[at].astype(jnp.float32) * right[at].astype(jnp.float32)).astype(o_buf.dtype)
        store(i).start()
    for i in range(blocks):
        store(i).wait()
    far.wait()


def apply_mix(left, right, stored):
    dma = pltpu.SemaphoreType.DMA
    scratch = [pltpu.VMEM(left.shape, left.dtype)] * 3 + [dma((2, 4)), dma(()), dma((4,))]
    piece = jax.ShapeDtypeStruct((*stored.shape[:2], left.shape[1]), stored.dtype)
    out = (jax.ShapeDtypeStruct(left.shape, left.dtype), piece)
    return call(mix_kernel, (left, right, stored), (), out, scratch, 62)


def apply_gate(restored, mixed, gate_out, bias):
    scratch = [pltpu.VMEM(mixed.shape, mixed.dtype), pltpu.SemaphoreType.DMA((4,))]
    out = jax.ShapeDtypeStruct(mixed.shape, mixed.dtype)
    return call(gate_kernel, (), (restored, mixed, gate_out, bias[None, :]), out, scratch, 8)


def exchange(array):
    return lax.all_to_all(array, "ctx", split_axis=0, concat_axis=0, tiled=True)


def body(gate_in, values, gate_out, bias, spectrum):
    devices = lax.axis_size("ctx")
    members = lax.axis_size("fsdp")
    rows, channels = gate_in.shape
    block = rows // devices
    length = 2 * rows * devices
    position = lax.axis_index("ctx")
    member = lax.axis_index("fsdp")

    def piece_for(stored, shift):
        target = lax.rem(member + shift, members)
        return lax.dynamic_slice_in_dim(stored, target * channels, channels, 2)

    def send(piece, shift):
        return lax.ppermute(piece, "fsdp", [(m, (m + shift) % members) for m in range(members)])

    mixed, far = apply_mix(gate_in, values, spectrum)
    mixed, far, later = lax.optimization_barrier((mixed, far, spectrum))
    stage = exchange(mixed.reshape(devices, block, channels))
    far = send(far, 2)
    near, last = piece_for(later, 1), piece_for(later, members - 1)
    pieces = (spectrum, send(near, 1), far, send(last, members - 1))

    cross = cross_table(devices, block, False)
    cross_back = cross_table(devices, block, True)
    local = local_table(position, devices, rows, block, False)
    local_back = local_table(position, devices, rows, block, True)

    spread = apply_cross(cross, stage.reshape(rows, channels), 1.0 / SPREAD)
    stage = exchange(spread.reshape(devices, 2 * block, channels))
    turned = apply_local(local, local_back, pieces, stage.reshape(devices, RADIX, -1, channels))
    stage = exchange(turned.reshape(devices, 2 * block, channels))
    folded = apply_fold(cross_back, stage.reshape(2 * rows, channels), 2.0 / (length * SPREAD))
    restored = exchange(folded.reshape(devices, block, channels)).reshape(rows, channels)
    return apply_gate(restored, mixed, gate_out, bias)


def solution(mesh):
    return jax.shard_map(
        body,
        mesh=mesh,
        in_specs=(
            P("ctx", "fsdp"),
            P("ctx", "fsdp"),
            P("ctx", "fsdp"),
            P("fsdp"),
            P(None, ("ctx", "fsdp"), None),
        ),
        out_specs=P("ctx", "fsdp"),
        check_vma=False,
    )
```

```python
import functools
import math

import jax
import jax.numpy as jnp
from jax import lax
from jax.experimental import pallas as pl
from jax.experimental.pallas import tpu as pltpu
from jax.sharding import PartitionSpec as P


LANES = 512
RADIX = 4
SPREAD = 1.624475


def cosine(step, modulus):
    half = modulus // 2
    centred = jnp.bitwise_and(step + half, modulus - 1) - half
    y = (modulus // 4 - jnp.abs(centred)).astype(jnp.float32) * (2.0 * math.pi / modulus)
    z = y * y
    series = 1.0 / 6227020800.0
    for term in (-1.0 / 39916800.0, 1.0 / 362880.0, -1.0 / 5040.0, 1.0 / 120.0, -1.0 / 6.0, 1.0):
        series = series * z + term
    return series * y


def message(index, block):
    fine = block // RADIX
    return index % fine * RADIX + index // (2 * fine) % RADIX, index // fine % 2


def cross_table(devices, block, transpose):
    wide = jnp.arange(2 * devices * block, dtype=jnp.int32)
    residue = wide // (2 * block)
    wide_row, part = message(wide, block)
    narrow = jnp.arange(devices * block, dtype=jnp.int32)
    place, narrow_row = narrow // block, narrow % block
    first = residue == 0
    rate = jnp.where(first, part * devices, residue)
    phase = jnp.where(first, 0, part * (devices // 2))
    if transpose:
        step = place[:, None] * rate[None, :] + phase[None, :]
        same = narrow_row[:, None] == wide_row[None, :]
    else:
        step = rate[:, None] * place[None, :] + phase[:, None]
        same = wide_row[:, None] == narrow_row[None, :]
    return jnp.where(same, cosine(step, 2 * devices) * SPREAD, 0.0).astype(jnp.bfloat16)


def local_table(position, devices, rows, block, transpose):
    length = 2 * devices * rows
    stride = 2 * devices
    fine = block // RADIX
    quart = rows // RADIX
    first = position == 0
    out = jnp.arange(4 * quart, dtype=jnp.int32)
    group, out_part, order = out // (2 * quart), out // quart % 2, out % quart
    rate = jnp.where(first, stride * order + group * devices, stride * (order + 2 * quart * group) + position)
    inp = jnp.arange(2 * devices * fine, dtype=jnp.int32)
    in_part = inp // fine % 2
    base = inp // (2 * fine) * block + inp % fine * RADIX
    in_phase = jnp.where(first, 0, in_part)
    side = jnp.where(first, group, 2)
    digit = jnp.arange(RADIX, dtype=jnp.int32)[:, None, None]
    quarter = length // 4
    if transpose:
        row = digit + base[None, :, None]
        step = row * rate[None, None, :] + quarter * (out_part[None, None, :] - in_phase[None, :, None])
        keep = (side[None, :] == 2) | (side[None, :] == in_part[:, None])
    else:
        row = digit + base[None, None, :]
        step = row * rate[None, :, None] + quarter * (out_part[None, :, None] - in_phase[None, None, :])
        keep = (side[:, None] == 2) | (side[:, None] == in_part[None, :])
    return jnp.where(keep[None], cosine(step, length), 0.0).astype(jnp.bfloat16)


def each_block(width, step):
    def go(i, carry):
        step(i, pl.ds(pl.multiple_of(i * LANES, LANES), LANES))
        return carry

    lax.fori_loop(0, width // LANES, go, 0)


def cross_kernel(scale, table_ref, x_ref, o_hbm, o_buf, o_sem):
    def store(i, cols):
        return pltpu.make_async_copy(o_buf.at[:, cols], o_hbm.at[:, cols], o_sem.at[i])

    def step(i, cols):
        acc = jnp.dot(table_ref[...], x_ref[:, cols], preferred_element_type=jnp.float32)
        o_buf[:, cols] = (acc * scale).astype(o_buf.dtype)
        store(i, cols).start()

    each_block(x_ref.shape[1], step)
    each_block(x_ref.shape[1], lambda i, cols: store(i, cols).wait())


def fold_kernel(scale, table_ref, x_ref, o_ref):
    def step(i, cols):
        acc = jnp.dot(table_ref[...], x_ref[:, cols], preferred_element_type=jnp.float32)
        o_ref[:, cols] = (acc * scale).astype(o_ref.dtype)

    each_block(x_ref.shape[1], step)


def local_kernel(
    m_hbm, g_hbm, own_hbm, near_hbm, far_hbm, last_hbm, x_hbm, o_hbm,
    m_ref, g_ref, r_ref, x_ref, o_ref, b_ref, m_sem, g_sem, r_sem, x_sem, o_sem,
):
    quart, width = r_ref.shape[2] // 2, r_ref.shape[3]
    first = lax.axis_index("ctx") == 0
    member = lax.axis_index("fsdp")
    members = r_ref.shape[0]

    forward = pltpu.make_async_copy(m_hbm, m_ref, m_sem)
    backward = pltpu.make_async_copy(g_hbm, g_ref, g_sem)

    def filters(i, cols):
        mine = pl.ds(pl.multiple_of(member * width + i * LANES, LANES), LANES)
        sources = [own_hbm.at[:, :, mine]] + [piece.at[:, :, cols] for piece in (near_hbm, far_hbm, last_hbm)]
        return [
            pltpu.make_async_copy(source, r_ref.at[shift, :, :, cols], r_sem.at[shift, i])
            for shift, source in enumerate(sources)
        ]

    def response(group, cols):
        here = jnp.where(first, 2 * group, group)
        there = jnp.where(first, 2 * group + 1, members - 1 - group)
        here = lax.rem(member + members - here, members)
        there = lax.rem(member + members - there, members)
        size = 2 * quart
        row = lax.broadcasted_iota(jnp.int32, (size, size), 0)
        col = lax.broadcasted_iota(jnp.int32, (size, size), 1)
        shifted = jnp.where(first, 1, 0) if group == 0 else 0
        mirror = jnp.where(row + col == size - 1 + shifted, 0.5, 0.0).astype(jnp.bfloat16)
        even = 0.5 * r_ref[here, 0, :, cols].astype(jnp.float32) + jnp.dot(
            mirror, r_ref[there, 0, :, cols], preferred_element_type=jnp.float32
        )
        odd = 0.5 * r_ref[here, 1, :, cols].astype(jnp.float32) - jnp.dot(
            mirror, r_ref[there, 1, :, cols], preferred_element_type=jnp.float32
        )
        return even, odd, there

    def incoming(i, cols):
        return pltpu.make_async_copy(x_hbm.at[:, :, :, cols], x_ref.at[:, :, :, cols], x_sem.at[i])

    def store(i, cols):
        return pltpu.make_async_copy(o_ref.at[:, :, :, cols], o_hbm.at[:, :, :, cols], o_sem.at[i])

    def start(copies):
        for copy in copies:
            copy.start()

    def wait(copies):
        for copy in copies:
            copy.wait()

    forward.start()
    for i in range(width // LANES):
        incoming(i, pl.ds(i * LANES, LANES)).start()
        start(filters(i, pl.ds(i * LANES, LANES)))
    backward.start()
    forward.wait()

    def ahead(i, cols):
        incoming(i, cols).wait()
        v = []
        for digit in range(RADIX):
            x = x_ref[:, digit, :, cols]
            x = x.reshape(-1, x.shape[-1])
            v.append(jnp.dot(m_ref[digit], x, preferred_element_type=jnp.float32))
        wait(filters(i, cols))
        sum02, sum13, gap02, gap13 = v[0] + v[2], v[1] + v[3], v[0] - v[2], v[1] - v[3]
        total = sum02 + sum13
        for group in range(2):
            even, odd, there = response(group, cols)
            if group == 0:
                lone = first & (lax.broadcasted_iota(jnp.int32, (8, LANES), 0) == 0)
                edge = jnp.where(lone, 0.5 * r_ref[there, 0, :8, cols].astype(jnp.float32), 0.0)
                edge = (sum02[:8] - sum13[:8]) * edge
            at = 2 * group * quart
            re, im = slice(at, at + quart), slice(at + quart, at + 2 * quart)
            parts = []
            for turn, (real, imag) in enumerate(
                ((total[re], total[im]), (gap02[re] + gap13[im], gap02[im] - gap13[re]))
            ):
                here = slice(turn * quart, (turn + 1) * quart)
                parts.append((real * even[here] - imag * odd[here], real * odd[here] + imag * even[here]))
            (r0, i0), (r1, i1) = parts
            for digit, (real, imag) in enumerate(
                ((r0 + r1, i0 + i1), (r0 - i1, i0 + r1), (r0 - r1, i0 - i1), (r0 + i1, i0 - r1))
            ):
                if group == 0:
                    top = real[:8] + edge if digit % 2 == 0 else real[:8] - edge
                    real = jnp.concatenate([top, real[8:]], axis=0)
                b_ref[digit, re, cols] = real.astype(b_ref.dtype)
                b_ref[digit, im, cols] = imag.astype(b_ref.dtype)

    def back(i, cols):
        for digit in range(RADIX):
            y = jnp.dot(g_ref[digit], b_ref[digit, :, cols], preferred_element_type=jnp.float32)
            o_ref[:, digit, :, cols] = y.reshape(o_ref.shape[0], o_ref.shape[2], -1).astype(o_ref.dtype)
        store(i, cols).start()

    each_block(width, ahead)
    backward.wait()
    each_block(width, back)
    each_block(width, lambda i, cols: store(i, cols).wait())


def gate_kernel(restored_ref, mixed_ref, gate_ref, bias_ref, o_hbm, o_buf, o_sem):
    rows = o_buf.shape[0] // o_sem.shape[0]
    bias = bias_ref[...]

    def store(i):
        at = pl.ds(i * rows, rows)
        return pltpu.make_async_copy(o_buf.at[at], o_hbm.at[at], o_sem.at[i])

    for i in range(o_sem.shape[0]):
        at = slice(i * rows, (i + 1) * rows)
        convolved = restored_ref[at].astype(jnp.float32) + bias * mixed_ref[at].astype(jnp.float32)
        o_buf[at] = (gate_ref[at].astype(jnp.float32) * convolved).astype(o_buf.dtype)
        store(i).start()
    for i in range(o_sem.shape[0]):
        store(i).wait()


def call(kernel, stored, near, out, scratch, grant):
    there = pl.BlockSpec(memory_space=pltpu.HBM)
    return pl.pallas_call(
        kernel,
        in_specs=[there] * len(stored) + [pl.BlockSpec(memory_space=pltpu.VMEM)] * len(near),
        out_specs=jax.tree.map(lambda _: there, out),
        out_shape=out,
        scratch_shapes=scratch,
        compiler_params=pltpu.CompilerParams(vmem_limit_bytes=grant << 20),
    )(*stored, *near)


def apply_cross(table, x, scale):
    out = jax.ShapeDtypeStruct((table.shape[0], x.shape[1]), jnp.bfloat16)
    scratch = [pltpu.VMEM(out.shape, out.dtype), pltpu.SemaphoreType.DMA((x.shape[1] // LANES,))]
    return call(functools.partial(cross_kernel, scale), (), (table, x), out, scratch, 12)


def apply_fold(table, x, scale):
    vmem = pl.BlockSpec(memory_space=pltpu.VMEM)
    return pl.pallas_call(
        functools.partial(fold_kernel, scale),
        in_specs=[vmem] * 2,
        out_specs=vmem,
        out_shape=jax.ShapeDtypeStruct((table.shape[0], x.shape[1]), jnp.bfloat16),
        name="fold",
        compiler_params=pltpu.CompilerParams(vmem_limit_bytes=12 << 20),
    )(table, x)


def apply_local(forward, backward, pieces, x):
    count = x.shape[-1] // LANES
    rows = forward.shape[1]
    dma = pltpu.SemaphoreType.DMA
    stored = pltpu.VMEM((len(pieces), *pieces[1].shape), x.dtype)
    scratch = [pltpu.VMEM(forward.shape, x.dtype), pltpu.VMEM(backward.shape, x.dtype), stored]
    scratch += [pltpu.VMEM(x.shape, x.dtype), pltpu.VMEM(x.shape, x.dtype)]
    scratch += [pltpu.VMEM((RADIX, rows, x.shape[-1]), x.dtype)]
    scratch += [dma(()), dma(()), dma((len(pieces), count)), dma((count,)), dma((count,))]
    out = jax.ShapeDtypeStruct(x.shape, x.dtype)
    return call(local_kernel, (forward, backward, *pieces, x), (), out, scratch, 62)


def mix_kernel(
    left_hbm, right_hbm, stored_hbm, o_hbm, far_hbm, left, right, o_buf, far_buf, in_sem, far_sem, o_sem
):
    blocks = o_sem.shape[0]
    rows = o_buf.shape[0] // blocks
    width = far_hbm.shape[2]
    target = lax.rem(lax.axis_index("fsdp") + 2, stored_hbm.shape[2] // width)

    def loads(i):
        at = pl.ds(i * rows, rows)
        return [
            pltpu.make_async_copy(left_hbm.at[at], left.at[at], in_sem.at[0, i]),
            pltpu.make_async_copy(right_hbm.at[at], right.at[at], in_sem.at[1, i]),
        ]

    def store(i):
        at = pl.ds(i * rows, rows)
        return pltpu.make_async_copy(o_buf.at[at], o_hbm.at[at], o_sem.at[i])

    for i in range(blocks):
        for load in loads(i):
            load.start()
    mine = pl.ds(pl.multiple_of(target * width, width), width)
    parts = range(far_buf.shape[0])
    taken = [pltpu.make_async_copy(stored_hbm.at[p, :, mine], far_buf.at[p], far_sem.at[0, p]) for p in parts]
    given = [pltpu.make_async_copy(far_buf.at[p], far_hbm.at[p], far_sem.at[1, p]) for p in parts]
    for copy in taken:
        copy.start()
    for i in range(blocks):
        for load in loads(i):
            load.wait()
        at = slice(i * rows, (i + 1) * rows)
        o_buf[at] = (left[at].astype(jnp.float32) * right[at].astype(jnp.float32)).astype(o_buf.dtype)
        store(i).start()
    for p in parts:
        taken[p].wait()
        given[p].start()
    for i in range(blocks):
        store(i).wait()
    for copy in given:
        copy.wait()


def apply_mix(left, right, stored):
    dma = pltpu.SemaphoreType.DMA
    piece = jax.ShapeDtypeStruct((*stored.shape[:2], left.shape[1]), stored.dtype)
    scratch = [pltpu.VMEM(left.shape, left.dtype)] * 3 + [pltpu.VMEM(piece.shape, piece.dtype)]
    scratch += [dma((2, 4)), dma((2, piece.shape[0])), dma((4,))]
    out = (jax.ShapeDtypeStruct(left.shape, left.dtype), piece)
    return call(mix_kernel, (left, right, stored), (), out, scratch, 62)


def apply_gate(restored, mixed, gate_out, bias):
    scratch = [pltpu.VMEM(mixed.shape, mixed.dtype), pltpu.SemaphoreType.DMA((4,))]
    out = jax.ShapeDtypeStruct(mixed.shape, mixed.dtype)
    return call(gate_kernel, (), (restored, mixed, gate_out, bias[None, :]), out, scratch, 8)


def exchange(array):
    return lax.all_to_all(array, "ctx", split_axis=0, concat_axis=0, tiled=True)


def body(gate_in, values, gate_out, bias, spectrum):
    devices = lax.axis_size("ctx")
    members = lax.axis_size("fsdp")
    rows, channels = gate_in.shape
    block = rows // devices
    length = 2 * rows * devices
    position = lax.axis_index("ctx")
    member = lax.axis_index("fsdp")

    def piece_for(stored, shift):
        target = lax.rem(member + shift, members)
        return lax.dynamic_slice_in_dim(stored, target * channels, channels, 2)

    def send(piece, shift):
        return lax.ppermute(piece, "fsdp", [(m, (m + shift) % members) for m in range(members)])

    mixed, far = apply_mix(gate_in, values, spectrum)
    mixed, far, later = lax.optimization_barrier((mixed, far, spectrum))
    stage = exchange(mixed.reshape(devices, block, channels))
    far = send(far, 2)
    near, last = piece_for(later, 1), piece_for(later, members - 1)
    pieces = (spectrum, send(near, 1), far, send(last, members - 1))

    cross = cross_table(devices, block, False)
    cross_back = cross_table(devices, block, True)
    local = local_table(position, devices, rows, block, False)
    local_back = local_table(position, devices, rows, block, True)

    spread = apply_cross(cross, stage.reshape(rows, channels), 1.0 / SPREAD)
    stage = exchange(spread.reshape(devices, 2 * block, channels))
    turned = apply_local(local, local_back, pieces, stage.reshape(devices, RADIX, -1, channels))
    stage = exchange(turned.reshape(devices, 2 * block, channels))
    folded = apply_fold(cross_back, stage.reshape(2 * rows, channels), 2.0 / (length * SPREAD))
    restored = exchange(folded.reshape(devices, block, channels)).reshape(rows, channels)
    return apply_gate(restored, mixed, gate_out, bias)


def solution(mesh):
    return jax.shard_map(
        body,
        mesh=mesh,
        in_specs=(
            P("ctx", "fsdp"),
            P("ctx", "fsdp"),
            P("ctx", "fsdp"),
            P("fsdp"),
            P(None, ("ctx", "fsdp"), None),
        ),
        out_specs=P("ctx", "fsdp"),
        check_vma=False,
    )
```

```python
import functools
import math

import jax
import jax.numpy as jnp
from jax import lax
from jax.experimental import pallas as pl
from jax.experimental.pallas import tpu as pltpu
from jax.sharding import PartitionSpec as P


LANES = 512
RADIX = 4
SPREAD = 1.624475


def cosine(step, modulus):
    half = modulus // 2
    centred = jnp.bitwise_and(step + half, modulus - 1) - half
    y = (modulus // 4 - jnp.abs(centred)).astype(jnp.float32) * (2.0 * math.pi / modulus)
    z = y * y
    series = 1.0 / 6227020800.0
    for term in (-1.0 / 39916800.0, 1.0 / 362880.0, -1.0 / 5040.0, 1.0 / 120.0, -1.0 / 6.0, 1.0):
        series = series * z + term
    return series * y


def message(index, block):
    fine = block // RADIX
    return index % fine * RADIX + index // (2 * fine) % RADIX, index // fine % 2


def cross_table(devices, block, transpose):
    wide = jnp.arange(2 * devices * block, dtype=jnp.int32)
    residue = wide // (2 * block)
    wide_row, part = message(wide, block)
    narrow = jnp.arange(devices * block, dtype=jnp.int32)
    place, narrow_row = narrow // block, narrow % block
    first = residue == 0
    rate = jnp.where(first, part * devices, residue)
    phase = jnp.where(first, 0, part * (devices // 2))
    if transpose:
        step = place[:, None] * rate[None, :] + phase[None, :]
        same = narrow_row[:, None] == wide_row[None, :]
    else:
        step = rate[:, None] * place[None, :] + phase[:, None]
        same = wide_row[:, None] == narrow_row[None, :]
    return jnp.where(same, cosine(step, 2 * devices) * SPREAD, 0.0).astype(jnp.bfloat16)


def local_table(position, devices, rows, block, transpose):
    length = 2 * devices * rows
    stride = 2 * devices
    fine = block // RADIX
    quart = rows // RADIX
    first = position == 0
    out = jnp.arange(4 * quart, dtype=jnp.int32)
    group, out_part, order = out // (2 * quart), out // quart % 2, out % quart
    rate = jnp.where(first, stride * order + group * devices, stride * (order + 2 * quart * group) + position)
    inp = jnp.arange(2 * devices * fine, dtype=jnp.int32)
    in_part = inp // fine % 2
    base = inp // (2 * fine) * block + inp % fine * RADIX
    in_phase = jnp.where(first, 0, in_part)
    side = jnp.where(first, group, 2)
    digit = jnp.arange(RADIX, dtype=jnp.int32)[:, None, None]
    quarter = length // 4
    if transpose:
        row = digit + base[None, :, None]
        step = row * rate[None, None, :] + quarter * (out_part[None, None, :] - in_phase[None, :, None])
        keep = (side[None, :] == 2) | (side[None, :] == in_part[:, None])
    else:
        row = digit + base[None, None, :]
        step = row * rate[None, :, None] + quarter * (out_part[None, :, None] - in_phase[None, None, :])
        keep = (side[:, None] == 2) | (side[:, None] == in_part[None, :])
    return jnp.where(keep[None], cosine(step, length), 0.0).astype(jnp.bfloat16)


def each_block(width, step):
    def go(i, carry):
        step(i, pl.ds(pl.multiple_of(i * LANES, LANES), LANES))
        return carry

    lax.fori_loop(0, width // LANES, go, 0)


def cross_kernel(scale, table_ref, x_ref, o_hbm, o_buf, o_sem):
    def store(i, cols):
        return pltpu.make_async_copy(o_buf.at[:, cols], o_hbm.at[:, cols], o_sem.at[i])

    def step(i, cols):
        acc = jnp.dot(table_ref[...], x_ref[:, cols], preferred_element_type=jnp.float32)
        o_buf[:, cols] = (acc * scale).astype(o_buf.dtype)
        store(i, cols).start()

    each_block(x_ref.shape[1], step)
    each_block(x_ref.shape[1], lambda i, cols: store(i, cols).wait())


def fold_kernel(scale, table_ref, x_ref, o_ref):
    def step(i, cols):
        acc = jnp.dot(table_ref[...], x_ref[:, cols], preferred_element_type=jnp.float32)
        o_ref[:, cols] = (acc * scale).astype(o_ref.dtype)

    each_block(x_ref.shape[1], step)


def local_kernel(
    m_hbm, g_hbm, own_hbm, near_hbm, far_hbm, last_hbm, x_hbm, o_hbm,
    m_ref, g_ref, r_ref, x_ref, o_ref, b_ref, mirrors, m_sem, g_sem, r_sem, x_sem, o_sem,
):
    quart, width = r_ref.shape[2] // 2, r_ref.shape[3]
    first = lax.axis_index("ctx") == 0
    member = lax.axis_index("fsdp")
    members = r_ref.shape[0]

    forward = pltpu.make_async_copy(m_hbm, m_ref, m_sem)
    backward = pltpu.make_async_copy(g_hbm, g_ref, g_sem)

    def filters(i, cols):
        mine = pl.ds(pl.multiple_of(member * width + i * LANES, LANES), LANES)
        sources = [own_hbm.at[:, :, mine]] + [piece.at[:, :, cols] for piece in (near_hbm, far_hbm, last_hbm)]
        return [
            pltpu.make_async_copy(source, r_ref.at[shift, :, :, cols], r_sem.at[shift, i])
            for shift, source in enumerate(sources)
        ]

    def response(group, cols):
        here = jnp.where(first, 2 * group, group)
        there = jnp.where(first, 2 * group + 1, members - 1 - group)
        here = lax.rem(member + members - here, members)
        there = lax.rem(member + members - there, members)
        mirror = mirrors[group]
        even = 0.5 * r_ref[here, 0, :, cols].astype(jnp.float32) + jnp.dot(
            mirror, r_ref[there, 0, :, cols], preferred_element_type=jnp.float32
        )
        odd = 0.5 * r_ref[here, 1, :, cols].astype(jnp.float32) - jnp.dot(
            mirror, r_ref[there, 1, :, cols], preferred_element_type=jnp.float32
        )
        return even, odd, there

    def incoming(i, cols):
        return pltpu.make_async_copy(x_hbm.at[:, :, :, cols], x_ref.at[:, :, :, cols], x_sem.at[i])

    def store(digit, i, cols):
        return pltpu.make_async_copy(o_ref.at[:, digit, :, cols], o_hbm.at[:, digit, :, cols], o_sem.at[digit, i])

    def start(copies):
        for copy in copies:
            copy.start()

    def wait(copies):
        for copy in copies:
            copy.wait()

    forward.start()
    for i in range(width // LANES):
        incoming(i, pl.ds(i * LANES, LANES)).start()
        start(filters(i, pl.ds(i * LANES, LANES)))
    backward.start()

    size = 2 * quart
    row = lax.broadcasted_iota(jnp.int32, (size, size), 0)
    col = lax.broadcasted_iota(jnp.int32, (size, size), 1)
    for group in range(2):
        shifted = jnp.where(first, 1, 0) if group == 0 else 0
        mirrors[group] = jnp.where(row + col == size - 1 + shifted, 0.5, 0.0).astype(mirrors.dtype)

    forward.wait()

    def ahead(i, cols):
        incoming(i, cols).wait()
        v = []
        for digit in range(RADIX):
            x = x_ref[:, digit, :, cols]
            x = x.reshape(-1, x.shape[-1])
            v.append(jnp.dot(m_ref[digit], x, preferred_element_type=jnp.float32))
        wait(filters(i, cols))
        sum02, sum13, gap02, gap13 = v[0] + v[2], v[1] + v[3], v[0] - v[2], v[1] - v[3]
        total = sum02 + sum13
        for group in range(2):
            even, odd, there = response(group, cols)
            if group == 0:
                lone = first & (lax.broadcasted_iota(jnp.int32, (8, LANES), 0) == 0)
                edge = jnp.where(lone, 0.5 * r_ref[there, 0, :8, cols].astype(jnp.float32), 0.0)
                edge = (sum02[:8] - sum13[:8]) * edge
            at = 2 * group * quart
            re, im = slice(at, at + quart), slice(at + quart, at + 2 * quart)
            parts = []
            for turn, (real, imag) in enumerate(
                ((total[re], total[im]), (gap02[re] + gap13[im], gap02[im] - gap13[re]))
            ):
                here = slice(turn * quart, (turn + 1) * quart)
                parts.append((real * even[here] - imag * odd[here], real * odd[here] + imag * even[here]))
            (r0, i0), (r1, i1) = parts
            for digit, (real, imag) in enumerate(
                ((r0 + r1, i0 + i1), (r0 - i1, i0 + r1), (r0 - r1, i0 - i1), (r0 + i1, i0 - r1))
            ):
                if group == 0:
                    top = real[:8] + edge if digit % 2 == 0 else real[:8] - edge
                    real = jnp.concatenate([top, real[8:]], axis=0)
                b_ref[digit, re, cols] = real.astype(b_ref.dtype)
                b_ref[digit, im, cols] = imag.astype(b_ref.dtype)

    def back(i, cols):
        for digit in range(RADIX):
            y = jnp.dot(g_ref[digit], b_ref[digit, :, cols], preferred_element_type=jnp.float32)
            o_ref[:, digit, :, cols] = y.reshape(o_ref.shape[0], o_ref.shape[2], -1).astype(o_ref.dtype)
            store(digit, i, cols).start()

    each_block(width, ahead)
    backward.wait()
    each_block(width, back)
    for digit in range(RADIX):
        each_block(width, lambda i, cols, digit=digit: store(digit, i, cols).wait())


def gate_kernel(restored_ref, mixed_ref, gate_ref, bias_ref, o_hbm, o_buf, o_sem):
    rows = o_buf.shape[0] // o_sem.shape[0]
    bias = bias_ref[...]

    def store(i):
        at = pl.ds(i * rows, rows)
        return pltpu.make_async_copy(o_buf.at[at], o_hbm.at[at], o_sem.at[i])

    for i in range(o_sem.shape[0]):
        at = slice(i * rows, (i + 1) * rows)
        convolved = restored_ref[at].astype(jnp.float32) + bias * mixed_ref[at].astype(jnp.float32)
        o_buf[at] = (gate_ref[at].astype(jnp.float32) * convolved).astype(o_buf.dtype)
        store(i).start()
    for i in range(o_sem.shape[0]):
        store(i).wait()


def call(kernel, stored, near, out, scratch, grant):
    there = pl.BlockSpec(memory_space=pltpu.HBM)
    return pl.pallas_call(
        kernel,
        in_specs=[there] * len(stored) + [pl.BlockSpec(memory_space=pltpu.VMEM)] * len(near),
        out_specs=jax.tree.map(lambda _: there, out),
        out_shape=out,
        scratch_shapes=scratch,
        compiler_params=pltpu.CompilerParams(vmem_limit_bytes=grant << 20),
    )(*stored, *near)


def apply_cross(table, x, scale):
    out = jax.ShapeDtypeStruct((table.shape[0], x.shape[1]), jnp.bfloat16)
    scratch = [pltpu.VMEM(out.shape, out.dtype), pltpu.SemaphoreType.DMA((x.shape[1] // LANES,))]
    return call(functools.partial(cross_kernel, scale), (), (table, x), out, scratch, 12)


def apply_fold(table, x, scale):
    vmem = pl.BlockSpec(memory_space=pltpu.VMEM)
    return pl.pallas_call(
        functools.partial(fold_kernel, scale),
        in_specs=[vmem] * 2,
        out_specs=vmem,
        out_shape=jax.ShapeDtypeStruct((table.shape[0], x.shape[1]), jnp.bfloat16),
        name="fold",
        compiler_params=pltpu.CompilerParams(vmem_limit_bytes=12 << 20),
    )(table, x)


def apply_local(forward, backward, pieces, x):
    count = x.shape[-1] // LANES
    rows = forward.shape[1]
    dma = pltpu.SemaphoreType.DMA
    stored = pltpu.VMEM((len(pieces), *pieces[1].shape), x.dtype)
    scratch = [pltpu.VMEM(forward.shape, x.dtype), pltpu.VMEM(backward.shape, x.dtype), stored]
    scratch += [pltpu.VMEM(x.shape, x.dtype), pltpu.VMEM(x.shape, x.dtype)]
    scratch += [pltpu.VMEM((RADIX, rows, x.shape[-1]), x.dtype), pltpu.VMEM((2, rows // 2, rows // 2), x.dtype)]
    scratch += [dma(()), dma(()), dma((len(pieces), count)), dma((count,)), dma((RADIX, count))]
    out = jax.ShapeDtypeStruct(x.shape, x.dtype)
    return call(local_kernel, (forward, backward, *pieces, x), (), out, scratch, 62)


def mix_kernel(
    left_hbm, right_hbm, stored_hbm, o_hbm, far_hbm, left, right, o_buf, far_buf, in_sem, far_sem, o_sem
):
    blocks = o_sem.shape[0]
    rows = o_buf.shape[0] // blocks
    width = far_hbm.shape[2]
    target = lax.rem(lax.axis_index("fsdp") + 2, stored_hbm.shape[2] // width)

    def loads(i):
        at = pl.ds(i * rows, rows)
        return [
            pltpu.make_async_copy(left_hbm.at[at], left.at[at], in_sem.at[0, i]),
            pltpu.make_async_copy(right_hbm.at[at], right.at[at], in_sem.at[1, i]),
        ]

    def store(i):
        at = pl.ds(i * rows, rows)
        return pltpu.make_async_copy(o_buf.at[at], o_hbm.at[at], o_sem.at[i])

    mine = pl.ds(pl.multiple_of(target * width, width), width)
    parts = range(far_buf.shape[0])
    taken = [pltpu.make_async_copy(stored_hbm.at[p, :, mine], far_buf.at[p], far_sem.at[0, p]) for p in parts]
    given = [pltpu.make_async_copy(far_buf.at[p], far_hbm.at[p], far_sem.at[1, p]) for p in parts]
    for copy in taken:
        copy.start()
    for i in range(blocks):
        for load in loads(i):
            load.start()
    for p in parts:
        taken[p].wait()
        given[p].start()
    for i in range(blocks):
        for load in loads(i):
            load.wait()
        at = slice(i * rows, (i + 1) * rows)
        o_buf[at] = (left[at].astype(jnp.float32) * right[at].astype(jnp.float32)).astype(o_buf.dtype)
        store(i).start()
    for i in range(blocks):
        store(i).wait()
    for copy in given:
        copy.wait()


def apply_mix(left, right, stored):
    dma = pltpu.SemaphoreType.DMA
    piece = jax.ShapeDtypeStruct((*stored.shape[:2], left.shape[1]), stored.dtype)
    scratch = [pltpu.VMEM(left.shape, left.dtype)] * 3 + [pltpu.VMEM(piece.shape, piece.dtype)]
    scratch += [dma((2, 4)), dma((2, piece.shape[0])), dma((4,))]
    out = (jax.ShapeDtypeStruct(left.shape, left.dtype), piece)
    return call(mix_kernel, (left, right, stored), (), out, scratch, 62)


def apply_gate(restored, mixed, gate_out, bias):
    scratch = [pltpu.VMEM(mixed.shape, mixed.dtype), pltpu.SemaphoreType.DMA((4,))]
    out = jax.ShapeDtypeStruct(mixed.shape, mixed.dtype)
    return call(gate_kernel, (), (restored, mixed, gate_out, bias[None, :]), out, scratch, 8)


def exchange(array):
    return lax.all_to_all(array, "ctx", split_axis=0, concat_axis=0, tiled=True)


def body(gate_in, values, gate_out, bias, spectrum):
    devices = lax.axis_size("ctx")
    members = lax.axis_size("fsdp")
    rows, channels = gate_in.shape
    block = rows // devices
    length = 2 * rows * devices
    position = lax.axis_index("ctx")
    member = lax.axis_index("fsdp")

    def piece_for(stored, shift):
        target = lax.rem(member + shift, members)
        return lax.dynamic_slice_in_dim(stored, target * channels, channels, 2)

    def send(piece, shift):
        return lax.ppermute(piece, "fsdp", [(m, (m + shift) % members) for m in range(members)])

    mixed, far = apply_mix(gate_in, values, spectrum)
    mixed, far, later = lax.optimization_barrier((mixed, far, spectrum))
    stage = exchange(mixed.reshape(devices, block, channels))
    far = send(far, 2)
    near, last = piece_for(later, 1), piece_for(later, members - 1)
    pieces = (spectrum, send(near, 1), far, send(last, members - 1))

    cross = cross_table(devices, block, False)
    cross_back = cross_table(devices, block, True)
    local = local_table(position, devices, rows, block, False)
    local_back = local_table(position, devices, rows, block, True)

    spread = apply_cross(cross, stage.reshape(rows, channels), 1.0 / SPREAD)
    stage = exchange(spread.reshape(devices, 2 * block, channels))
    turned = apply_local(local, local_back, pieces, stage.reshape(devices, RADIX, -1, channels))
    stage = exchange(turned.reshape(devices, 2 * block, channels))
    folded = apply_fold(cross_back, stage.reshape(2 * rows, channels), 2.0 / (length * SPREAD))
    restored = exchange(folded.reshape(devices, block, channels)).reshape(rows, channels)
    return apply_gate(restored, mixed, gate_out, bias)


def solution(mesh):
    return jax.shard_map(
        body,
        mesh=mesh,
        in_specs=(
            P("ctx", "fsdp"),
            P("ctx", "fsdp"),
            P("ctx", "fsdp"),
            P("fsdp"),
            P(None, ("ctx", "fsdp"), None),
        ),
        out_specs=P("ctx", "fsdp"),
        check_vma=False,
    )
```

```python
import functools
import math

import jax
import jax.numpy as jnp
from jax import lax
from jax.experimental import pallas as pl
from jax.experimental.pallas import tpu as pltpu
from jax.sharding import PartitionSpec as P


LANES = 512
RADIX = 4
SPREAD = 1.624475


def cosine(step, modulus):
    half = modulus // 2
    centred = jnp.bitwise_and(step + half, modulus - 1) - half
    y = (modulus // 4 - jnp.abs(centred)).astype(jnp.float32) * (2.0 * math.pi / modulus)
    z = y * y
    series = 1.0 / 6227020800.0
    for term in (-1.0 / 39916800.0, 1.0 / 362880.0, -1.0 / 5040.0, 1.0 / 120.0, -1.0 / 6.0, 1.0):
        series = series * z + term
    return series * y


def message(index, block):
    fine = block // RADIX
    return index % fine * RADIX + index // (2 * fine) % RADIX, index // fine % 2


def cross_table(devices, block, transpose):
    wide = jnp.arange(2 * devices * block, dtype=jnp.int32)
    residue = wide // (2 * block)
    wide_row, part = message(wide, block)
    narrow = jnp.arange(devices * block, dtype=jnp.int32)
    place, narrow_row = narrow // block, narrow % block
    first = residue == 0
    rate = jnp.where(first, part * devices, residue)
    phase = jnp.where(first, 0, part * (devices // 2))
    if transpose:
        step = place[:, None] * rate[None, :] + phase[None, :]
        same = narrow_row[:, None] == wide_row[None, :]
    else:
        step = rate[:, None] * place[None, :] + phase[:, None]
        same = wide_row[:, None] == narrow_row[None, :]
    return jnp.where(same, cosine(step, 2 * devices) * SPREAD, 0.0).astype(jnp.bfloat16)


def local_table(position, devices, rows, block, transpose):
    length = 2 * devices * rows
    stride = 2 * devices
    fine = block // RADIX
    quart = rows // RADIX
    first = position == 0
    out = jnp.arange(4 * quart, dtype=jnp.int32)
    group, out_part, order = out // (2 * quart), out // quart % 2, out % quart
    rate = jnp.where(first, stride * order + group * devices, stride * (order + 2 * quart * group) + position)
    inp = jnp.arange(2 * devices * fine, dtype=jnp.int32)
    in_part = inp // fine % 2
    base = inp // (2 * fine) * block + inp % fine * RADIX
    in_phase = jnp.where(first, 0, in_part)
    side = jnp.where(first, group, 2)
    digit = jnp.arange(RADIX, dtype=jnp.int32)[:, None, None]
    quarter = length // 4
    if transpose:
        row = digit + base[None, :, None]
        step = row * rate[None, None, :] + quarter * (out_part[None, None, :] - in_phase[None, :, None])
        keep = (side[None, :] == 2) | (side[None, :] == in_part[:, None])
    else:
        row = digit + base[None, None, :]
        step = row * rate[None, :, None] + quarter * (out_part[None, :, None] - in_phase[None, None, :])
        keep = (side[:, None] == 2) | (side[:, None] == in_part[None, :])
    return jnp.where(keep[None], cosine(step, length), 0.0).astype(jnp.bfloat16)


def each_block(width, step):
    def go(i, carry):
        step(i, pl.ds(pl.multiple_of(i * LANES, LANES), LANES))
        return carry

    lax.fori_loop(0, width // LANES, go, 0)


def cross_kernel(scale, table_ref, x_ref, o_hbm, o_buf, o_sem):
    halves = o_sem.shape[0]
    half = o_buf.shape[0] // halves

    def store(h, i, cols):
        rows = pl.ds(h * half, half)
        return pltpu.make_async_copy(o_buf.at[rows, cols], o_hbm.at[rows, cols], o_sem.at[h, i])

    def step(i, cols):
        for h in range(halves):
            rows = pl.ds(h * half, half)
            acc = jnp.dot(table_ref[rows], x_ref[:, cols], preferred_element_type=jnp.float32)
            o_buf[rows, cols] = (acc * scale).astype(o_buf.dtype)
            store(h, i, cols).start()

    each_block(x_ref.shape[1], step)
    for h in range(halves):
        each_block(x_ref.shape[1], lambda i, cols, h=h: store(h, i, cols).wait())


def fold_kernel(scale, table_ref, x_ref, o_ref):
    def step(i, cols):
        acc = jnp.dot(table_ref[...], x_ref[:, cols], preferred_element_type=jnp.float32)
        o_ref[:, cols] = (acc * scale).astype(o_ref.dtype)

    each_block(x_ref.shape[1], step)


def local_kernel(
    m_hbm, g_hbm, own_hbm, near_hbm, far_hbm, last_hbm, x_hbm, o_hbm,
    m_ref, g_ref, r_ref, x_ref, o_ref, b_ref, mirrors, m_sem, g_sem, r_sem, x_sem, o_sem,
):
    quart, width = r_ref.shape[2] // 2, r_ref.shape[3]
    first = lax.axis_index("ctx") == 0
    member = lax.axis_index("fsdp")
    members = r_ref.shape[0]

    forward = pltpu.make_async_copy(m_hbm, m_ref, m_sem)
    backward = pltpu.make_async_copy(g_hbm, g_ref, g_sem)

    def filters(i, cols):
        mine = pl.ds(pl.multiple_of(member * width + i * LANES, LANES), LANES)
        sources = [own_hbm.at[:, :, mine]] + [piece.at[:, :, cols] for piece in (near_hbm, far_hbm, last_hbm)]
        return [
            pltpu.make_async_copy(source, r_ref.at[shift, :, :, cols], r_sem.at[shift, i])
            for shift, source in enumerate(sources)
        ]

    def response(group, cols):
        here = jnp.where(first, 2 * group, group)
        there = jnp.where(first, 2 * group + 1, members - 1 - group)
        here = lax.rem(member + members - here, members)
        there = lax.rem(member + members - there, members)
        mirror = mirrors[group]
        even = 0.5 * r_ref[here, 0, :, cols].astype(jnp.float32) + jnp.dot(
            mirror, r_ref[there, 0, :, cols], preferred_element_type=jnp.float32
        )
        odd = 0.5 * r_ref[here, 1, :, cols].astype(jnp.float32) - jnp.dot(
            mirror, r_ref[there, 1, :, cols], preferred_element_type=jnp.float32
        )
        return even, odd, there

    def incoming(i, cols):
        return pltpu.make_async_copy(x_hbm.at[:, :, :, cols], x_ref.at[:, :, :, cols], x_sem.at[i])

    def store(digit, i, cols):
        return pltpu.make_async_copy(o_ref.at[:, digit, :, cols], o_hbm.at[:, digit, :, cols], o_sem.at[digit, i])

    def start(copies):
        for copy in copies:
            copy.start()

    def wait(copies):
        for copy in copies:
            copy.wait()

    forward.start()
    for i in range(width // LANES):
        incoming(i, pl.ds(i * LANES, LANES)).start()
        start(filters(i, pl.ds(i * LANES, LANES)))
    backward.start()

    size = 2 * quart
    row = lax.broadcasted_iota(jnp.int32, (size, size), 0)
    col = lax.broadcasted_iota(jnp.int32, (size, size), 1)
    for group in range(2):
        shifted = jnp.where(first, 1, 0) if group == 0 else 0
        mirrors[group] = jnp.where(row + col == size - 1 + shifted, 0.5, 0.0).astype(mirrors.dtype)

    forward.wait()

    def ahead(i, cols):
        incoming(i, cols).wait()
        v = []
        for digit in range(RADIX):
            x = x_ref[:, digit, :, cols]
            x = x.reshape(-1, x.shape[-1])
            v.append(jnp.dot(m_ref[digit], x, preferred_element_type=jnp.float32))
        wait(filters(i, cols))
        sum02, sum13, gap02, gap13 = v[0] + v[2], v[1] + v[3], v[0] - v[2], v[1] - v[3]
        total = sum02 + sum13
        for group in range(2):
            even, odd, there = response(group, cols)
            if group == 0:
                lone = first & (lax.broadcasted_iota(jnp.int32, (8, LANES), 0) == 0)
                edge = jnp.where(lone, 0.5 * r_ref[there, 0, :8, cols].astype(jnp.float32), 0.0)
                edge = (sum02[:8] - sum13[:8]) * edge
            at = 2 * group * quart
            re, im = slice(at, at + quart), slice(at + quart, at + 2 * quart)
            parts = []
            for turn, (real, imag) in enumerate(
                ((total[re], total[im]), (gap02[re] + gap13[im], gap02[im] - gap13[re]))
            ):
                here = slice(turn * quart, (turn + 1) * quart)
                parts.append((real * even[here] - imag * odd[here], real * odd[here] + imag * even[here]))
            (r0, i0), (r1, i1) = parts
            for digit, (real, imag) in enumerate(
                ((r0 + r1, i0 + i1), (r0 - i1, i0 + r1), (r0 - r1, i0 - i1), (r0 + i1, i0 - r1))
            ):
                if group == 0:
                    top = real[:8] + edge if digit % 2 == 0 else real[:8] - edge
                    real = jnp.concatenate([top, real[8:]], axis=0)
                b_ref[digit, re, cols] = real.astype(b_ref.dtype)
                b_ref[digit, im, cols] = imag.astype(b_ref.dtype)

    def back(i, cols):
        for digit in range(RADIX):
            y = jnp.dot(g_ref[digit], b_ref[digit, :, cols], preferred_element_type=jnp.float32)
            o_ref[:, digit, :, cols] = y.reshape(o_ref.shape[0], o_ref.shape[2], -1).astype(o_ref.dtype)
            store(digit, i, cols).start()

    each_block(width, ahead)
    backward.wait()
    each_block(width, back)
    for digit in range(RADIX):
        each_block(width, lambda i, cols, digit=digit: store(digit, i, cols).wait())


def gate_kernel(restored_ref, mixed_ref, gate_ref, bias_ref, o_hbm, o_buf, o_sem):
    rows = o_buf.shape[0] // o_sem.shape[0]
    bias = bias_ref[...]

    def store(i):
        at = pl.ds(i * rows, rows)
        return pltpu.make_async_copy(o_buf.at[at], o_hbm.at[at], o_sem.at[i])

    for i in range(o_sem.shape[0]):
        at = slice(i * rows, (i + 1) * rows)
        convolved = restored_ref[at].astype(jnp.float32) + bias * mixed_ref[at].astype(jnp.float32)
        o_buf[at] = (gate_ref[at].astype(jnp.float32) * convolved).astype(o_buf.dtype)
        store(i).start()
    for i in range(o_sem.shape[0]):
        store(i).wait()


def call(kernel, stored, near, out, scratch, grant):
    there = pl.BlockSpec(memory_space=pltpu.HBM)
    return pl.pallas_call(
        kernel,
        in_specs=[there] * len(stored) + [pl.BlockSpec(memory_space=pltpu.VMEM)] * len(near),
        out_specs=jax.tree.map(lambda _: there, out),
        out_shape=out,
        scratch_shapes=scratch,
        compiler_params=pltpu.CompilerParams(vmem_limit_bytes=grant << 20),
    )(*stored, *near)


def apply_cross(table, x, scale):
    out = jax.ShapeDtypeStruct((table.shape[0], x.shape[1]), jnp.bfloat16)
    scratch = [pltpu.VMEM(out.shape, out.dtype), pltpu.SemaphoreType.DMA((2, x.shape[1] // LANES))]
    return call(functools.partial(cross_kernel, scale), (), (table, x), out, scratch, 12)


def apply_fold(table, x, scale):
    vmem = pl.BlockSpec(memory_space=pltpu.VMEM)
    return pl.pallas_call(
        functools.partial(fold_kernel, scale),
        in_specs=[vmem] * 2,
        out_specs=vmem,
        out_shape=jax.ShapeDtypeStruct((table.shape[0], x.shape[1]), jnp.bfloat16),
        name="fold",
        compiler_params=pltpu.CompilerParams(vmem_limit_bytes=12 << 20),
    )(table, x)


def apply_local(forward, backward, pieces, x):
    count = x.shape[-1] // LANES
    rows = forward.shape[1]
    dma = pltpu.SemaphoreType.DMA
    stored = pltpu.VMEM((len(pieces), *pieces[1].shape), x.dtype)
    scratch = [pltpu.VMEM(forward.shape, x.dtype), pltpu.VMEM(backward.shape, x.dtype), stored]
    scratch += [pltpu.VMEM(x.shape, x.dtype), pltpu.VMEM(x.shape, x.dtype)]
    scratch += [pltpu.VMEM((RADIX, rows, x.shape[-1]), x.dtype), pltpu.VMEM((2, rows // 2, rows // 2), x.dtype)]
    scratch += [dma(()), dma(()), dma((len(pieces), count)), dma((count,)), dma((RADIX, count))]
    out = jax.ShapeDtypeStruct(x.shape, x.dtype)
    return call(local_kernel, (forward, backward, *pieces, x), (), out, scratch, 62)


def mix_kernel(
    left_hbm, right_hbm, stored_hbm, o_hbm, far_hbm, left, right, o_buf, far_buf, in_sem, far_sem, o_sem
):
    blocks = o_sem.shape[0]
    rows = o_buf.shape[0] // blocks
    width = far_hbm.shape[2]
    target = lax.rem(lax.axis_index("fsdp") + 2, stored_hbm.shape[2] // width)

    def loads(i):
        at = pl.ds(i * rows, rows)
        return [
            pltpu.make_async_copy(left_hbm.at[at], left.at[at], in_sem.at[0, i]),
            pltpu.make_async_copy(right_hbm.at[at], right.at[at], in_sem.at[1, i]),
        ]

    def store(i):
        at = pl.ds(i * rows, rows)
        return pltpu.make_async_copy(o_buf.at[at], o_hbm.at[at], o_sem.at[i])

    for i in range(blocks):
        for load in loads(i):
            load.start()
    mine = pl.ds(pl.multiple_of(target * width, width), width)
    parts = range(far_buf.shape[0])
    taken = [pltpu.make_async_copy(stored_hbm.at[p, :, mine], far_buf.at[p], far_sem.at[0, p]) for p in parts]
    given = [pltpu.make_async_copy(far_buf.at[p], far_hbm.at[p], far_sem.at[1, p]) for p in parts]
    for copy in taken:
        copy.start()
    for i in range(blocks):
        for load in loads(i):
            load.wait()
        at = slice(i * rows, (i + 1) * rows)
        o_buf[at] = (left[at].astype(jnp.float32) * right[at].astype(jnp.float32)).astype(o_buf.dtype)
        store(i).start()
    for p in parts:
        taken[p].wait()
        given[p].start()
    for i in range(blocks):
        store(i).wait()
    for copy in given:
        copy.wait()


def apply_mix(left, right, stored):
    dma = pltpu.SemaphoreType.DMA
    piece = jax.ShapeDtypeStruct((*stored.shape[:2], left.shape[1]), stored.dtype)
    scratch = [pltpu.VMEM(left.shape, left.dtype)] * 3 + [pltpu.VMEM(piece.shape, piece.dtype)]
    scratch += [dma((2, 4)), dma((2, piece.shape[0])), dma((4,))]
    out = (jax.ShapeDtypeStruct(left.shape, left.dtype), piece)
    return call(mix_kernel, (left, right, stored), (), out, scratch, 62)


def apply_gate(restored, mixed, gate_out, bias):
    scratch = [pltpu.VMEM(mixed.shape, mixed.dtype), pltpu.SemaphoreType.DMA((4,))]
    out = jax.ShapeDtypeStruct(mixed.shape, mixed.dtype)
    return call(gate_kernel, (), (restored, mixed, gate_out, bias[None, :]), out, scratch, 8)


def exchange(array):
    return lax.all_to_all(array, "ctx", split_axis=0, concat_axis=0, tiled=True)


def body(gate_in, values, gate_out, bias, spectrum):
    devices = lax.axis_size("ctx")
    members = lax.axis_size("fsdp")
    rows, channels = gate_in.shape
    block = rows // devices
    length = 2 * rows * devices
    position = lax.axis_index("ctx")
    member = lax.axis_index("fsdp")

    def piece_for(stored, shift):
        target = lax.rem(member + shift, members)
        return lax.dynamic_slice_in_dim(stored, target * channels, channels, 2)

    def send(piece, shift):
        return lax.ppermute(piece, "fsdp", [(m, (m + shift) % members) for m in range(members)])

    mixed, far = apply_mix(gate_in, values, spectrum)
    mixed, far, later = lax.optimization_barrier((mixed, far, spectrum))
    stage = exchange(mixed.reshape(devices, block, channels))
    far = send(far, 2)
    near, last = piece_for(later, 1), piece_for(later, members - 1)
    pieces = (spectrum, send(near, 1), far, send(last, members - 1))

    cross = cross_table(devices, block, False)
    cross_back = cross_table(devices, block, True)
    local = local_table(position, devices, rows, block, False)
    local_back = local_table(position, devices, rows, block, True)

    spread = apply_cross(cross, stage.reshape(rows, channels), 1.0 / SPREAD)
    stage = exchange(spread.reshape(devices, 2 * block, channels))
    turned = apply_local(local, local_back, pieces, stage.reshape(devices, RADIX, -1, channels))
    stage = exchange(turned.reshape(devices, 2 * block, channels))
    folded = apply_fold(cross_back, stage.reshape(2 * rows, channels), 2.0 / (length * SPREAD))
    restored = exchange(folded.reshape(devices, block, channels)).reshape(rows, channels)
    return apply_gate(restored, mixed, gate_out, bias)


def solution(mesh):
    return jax.shard_map(
        body,
        mesh=mesh,
        in_specs=(
            P("ctx", "fsdp"),
            P("ctx", "fsdp"),
            P("ctx", "fsdp"),
            P("fsdp"),
            P(None, ("ctx", "fsdp"), None),
        ),
        out_specs=P("ctx", "fsdp"),
        check_vma=False,
    )
```
